32 devices in a mesh: row: 8 (over y, x, core), col: 4 (over z).
Axes of the slice: x: 2, y: 2, z: 4, core: 2. Of those that a mesh axis runs over, the one named last changes fastest.
Arguments:
- vectors: bfloat16 [4, 16384], P(None, ('row', 'col')), may hold values from -6 to 6
- tile_values: bfloat16 [8, 4, 32, 4096], P('row', 'col'), may hold values from -0.75 to 0.75
- tile_rows: int32 [8, 4, 32], P('row', 'col'), may hold values from 0 to 31, as said below
- tile_cols: int32 [8, 4, 32], P('row', 'col'), may hold values from 0 to 63
- tile_scale: int32 [8, 4, 32], P('row', 'col'), may hold values from 0 to 63
- tile_count: int32 [8, 4], P('row', 'col'), may hold values from 2 to 32, as said below
- scale_table: float32 [64], replicated, may hold values from 0.1 to 1.5
Outputs:
- product: float32 [4, 16384], P(None, ('row', 'col'))
The draws below stay inside these ranges and needn't reach their ends.
Inputs may be any that keep to these rules, and one draw needn't show every extreme that they name: Slots 0 to tile_count - 1 of a device hold its tiles, later slots are ignored; some device has all 32 slots live. On device (r, c), each slot t below min(8, 2) holds a diagonal block: tile_rows[r, c, t] = c * 8 + t; the other slots are uniform over the range.
All inputs are finite; a program needn't handle non-finite values.
Results may differ from the reference program's by a relative error of at most 0.0003.
Values may be sent and summed in bfloat16 or wider, within the bound.
A program may use at most 64 MiB of HBM per device.

```python
import math
import jax
import jax.numpy as jnp
from jax import lax

TILE = 64
NVEC = 4
NSCALE = 64
V = 512
TILES_DEV = 32
GRID_ROWS = 8
GRID_COLS = 4
NV = 16384
N_ROW = 8
N_COL = 4


def diagonal_slots():
    return min(V // TILE, TILES_DEV // 16)


def draw_tile_rows(key, part):
    diag_count = diagonal_slots()
    random_rows = jax.random.randint(jax.random.fold_in(key, 11), (GRID_ROWS, GRID_COLS, TILES_DEV), 0, GRID_COLS * V // TILE)
    col_place = jnp.arange(GRID_COLS, dtype=jnp.int32)[None, :, None]
    slot_place = jnp.arange(TILES_DEV, dtype=jnp.int32)[None, None, :]
    own_blocks = col_place * (V // TILE) + slot_place
    return jnp.where(slot_place < diag_count, own_blocks, random_rows).astype(jnp.int32)


def draw_tile_cols(key, part):
    diag_count = diagonal_slots()
    random_cols = jax.random.randint(jax.random.fold_in(key, 13), (GRID_ROWS, GRID_COLS, TILES_DEV), 0, GRID_ROWS * V // TILE)
    row_place = jnp.arange(GRID_ROWS, dtype=jnp.int32)[:, None, None]
    slot_place = jnp.arange(TILES_DEV, dtype=jnp.int32)[None, None, :]
    own_blocks = row_place * (V // TILE) + slot_place
    return jnp.where(slot_place < diag_count, own_blocks, random_cols).astype(jnp.int32)


def draw_tile_count(key, part):
    split_keys = jax.random.split(jax.random.fold_in(key, 7), 3)
    heavy_mask = jax.random.randint(split_keys[0], (GRID_ROWS, GRID_COLS), 0, 8) == 0
    light_load = jax.random.randint(split_keys[1], (GRID_ROWS, GRID_COLS), TILES_DEV // 16, TILES_DEV // 2 + 1)
    slot_counts = jnp.where(heavy_mask, TILES_DEV, light_load).reshape(-1)
    chosen_one = jax.random.randint(split_keys[2], (), 0, GRID_ROWS * GRID_COLS)
    slot_counts = slot_counts.at[chosen_one].set(TILES_DEV)
    return slot_counts.reshape(GRID_ROWS, GRID_COLS).astype(jnp.int32)


def touch_ends(result, rng, low, largest):
    dims = result.shape
    index_at = [jax.random.randint(jax.random.fold_in(rng, axis), (), 0, dims[axis]) for axis in range(len(dims))]
    result = result.at[tuple(index_at)].set(low)
    longest = dims.index(max(dims))
    index_at[longest] = (index_at[longest] + 1) % dims[longest]
    return result.at[tuple(index_at)].set(largest)


def shard_levels(stream_key, dims, cuts, smallest, top_value):
    def one(dim, shards_of):
        heights = jax.random.uniform(jax.random.fold_in(jax.random.fold_in(stream_key, 6), dim), (shards_of,), jnp.float32, smallest / len(cuts), top_value / len(cuts))
        return jnp.repeat(jnp.exp(heights), dims[dim] // shards_of).reshape((-1,) + (1,) * (len(dims) - dim - 1))

    loudness = one(*cuts[0])
    for cut in cuts[1:]:
        loudness = loudness * one(*cut)
    return loudness


def scatter_about(rng, shape, width, most, cuts=(), kind=jnp.bfloat16):
    array = jax.random.normal(rng, shape, jnp.float32) * width
    if len(cuts) > 0:
        array = shard_levels(rng, shape, cuts, -0.22, 0.18) * array
    return jnp.clip(array, min=-most, max=most).astype(kind)


def setup_inputs(seed: int = 0) -> dict:
    streams_of = jax.random.split(jax.random.key(seed), 8)
    vectors = scatter_about(streams_of[0], (NVEC, NV), 1.0, 6.0, ((1, 32),))
    tile_values = scatter_about(streams_of[1], (GRID_ROWS, GRID_COLS, TILES_DEV, TILE * TILE), TILE ** -0.5, 0.75, ((0, 8), (1, 4)))
    tile_rows = draw_tile_rows(jax.random.fold_in(streams_of[7], 71), 0)
    tile_cols = draw_tile_cols(jax.random.fold_in(streams_of[7], 71), 0)
    tile_scale = touch_ends(jax.random.randint(streams_of[4], (GRID_ROWS, GRID_COLS, TILES_DEV), 0, NSCALE), jax.random.fold_in(streams_of[4], 1), 0, NSCALE - 1).astype(jnp.int32)
    tile_count = draw_tile_count(jax.random.fold_in(streams_of[7], 71), 0)
    scale_table = jnp.clip(jnp.exp(jax.random.uniform(streams_of[6], (NSCALE,), jnp.float32, math.log(0.1), math.log(1.5))), 0.1, 1.5)
    return dict(vectors=vectors, tile_values=tile_values, tile_rows=tile_rows, tile_cols=tile_cols, tile_scale=tile_scale, tile_count=tile_count, scale_table=scale_table)


def block_weights(row_ids, col_ids, scale_ids, live_count, scale_table, row_index, col_index, piece_blocks, col_total):
    global_row = row_index * col_total * piece_blocks + row_ids
    global_col = ((col_ids // piece_blocks) * col_total + col_index) * piece_blocks + col_ids % piece_blocks
    looked = jnp.take(scale_table, scale_ids)
    halved = jnp.where(global_row == global_col, 0.5, 1.0) * looked
    is_live = jnp.arange(row_ids.shape[0], dtype=jnp.int32) < live_count
    return jnp.where(is_live, halved, 0.0).astype(jnp.float32)


def tile_sums(row_vec, col_vec, values, row_ids, col_ids, weight_of, row_start, col_start):
    matrices = values.reshape(-1, TILE, TILE).astype(jnp.float32)
    near = jnp.take(row_vec, row_ids, axis=1).astype(jnp.float32)
    distant = jnp.take(col_vec, col_ids, axis=1).astype(jnp.float32)
    forward = jnp.einsum("tij,ktj->kti", matrices, distant) * weight_of[None, :, None]
    mirrored = jnp.einsum("tij,kti->ktj", matrices, near) * weight_of[None, :, None]
    return row_start.at[:, row_ids].add(forward), col_start.at[:, col_ids].add(mirrored)


def reference(vectors, tile_values, tile_rows, tile_cols, tile_scale, tile_count, scale_table):
    piece_blocks = V // TILE
    row_blocks = N_COL * piece_blocks
    col_blocks = N_ROW * piece_blocks
    device_total = N_ROW * N_COL
    grid = vectors.reshape(NVEC, N_ROW, N_COL, V)

    def per_device(items):
        device, values, row_ids, col_ids, scale_ids, live_count = items
        row_index = device // N_COL
        col_index = device % N_COL
        row_vec = lax.dynamic_index_in_dim(grid, row_index, 1, keepdims=False).reshape(NVEC, row_blocks, TILE)
        col_vec = lax.dynamic_index_in_dim(grid, col_index, 2, keepdims=False).reshape(NVEC, col_blocks, TILE)
        weight_of = block_weights(row_ids, col_ids, scale_ids, live_count, scale_table, row_index, col_index, piece_blocks, N_COL)
        row_start = jnp.zeros((NVEC, row_blocks, TILE), jnp.float32)
        col_start = jnp.zeros((NVEC, col_blocks, TILE), jnp.float32)
        return tile_sums(row_vec, col_vec, values, row_ids, col_ids, weight_of, row_start, col_start)

    devices = jnp.arange(device_total, dtype=jnp.int32)
    row_part, col_part = lax.map(per_device, (
        devices,
        tile_values.reshape(device_total, TILES_DEV, TILE * TILE),
        tile_rows.reshape(device_total, TILES_DEV),
        tile_cols.reshape(device_total, TILES_DEV),
        tile_scale.reshape(device_total, TILES_DEV),
        tile_count.reshape(device_total)))
    row_total = row_part.reshape(N_ROW, N_COL, NVEC, N_COL * V).sum(axis=1)
    row_total = jnp.transpose(row_total, (1, 0, 2)).reshape(NVEC, N_ROW * N_COL * V)
    col_total = col_part.reshape(N_ROW, N_COL, NVEC, N_ROW, V).sum(axis=0)
    col_total = jnp.transpose(col_total, (1, 2, 0, 3)).reshape(NVEC, N_ROW * N_COL * V)
    return row_total + col_total
```

```python
import functools

import jax
import jax.numpy as jnp
from jax import lax
from jax.experimental import pallas as pl
from jax.experimental.pallas import tpu as pltpu
from jax.sharding import PartitionSpec as P

TILE = 64
NVEC = 4
LANES = 128
GROUP = 4
MESH = pl.DeviceIdType.MESH


def relayout(slots, tv_vm, w32_vm, w_vm):
    pack = LANES // TILE
    step = max(1, 2 * LANES // (pack * slots))
    depth = pack * step * slots
    r = lax.broadcasted_iota(jnp.int32, (depth, depth), 0)
    c = lax.broadcasted_iota(jnp.int32, (depth, depth), 1)
    slot, i = lax.div(r, pack * step), lax.rem(r, pack * step)
    source = (lax.rem(i, pack) * step + lax.div(i, pack)) * slots + slot
    order = jnp.where(c == source, 1.0, 0.0).astype(jnp.bfloat16)
    low_half = lax.broadcasted_iota(jnp.int32, (slots, LANES), 1) < TILE
    total = TILE * TILE // LANES
    for first in range(0, total, step):
        low, high = [], []
        for g in range(first, first + step):
            part = tv_vm[:, g * LANES:(g + 1) * LANES].astype(jnp.float32)
            turned = pltpu.roll(part, TILE, 1)
            low.append(jnp.where(low_half, part, turned).astype(jnp.bfloat16))
            high.append(jnp.where(low_half, turned, part).astype(jnp.bfloat16))
        moved = jnp.dot(
            order, jnp.concatenate(low + high, axis=0), preferred_element_type=jnp.float32)
        w32_vm[:, first * pack:(first + step) * pack, :] = moved.reshape(
            slots, pack * step, LANES)
    w_vm[...] = w32_vm[...].reshape(slots * TILE, LANES).astype(jnp.bfloat16)


def kernel(
    n_row, n_col, slots, piece_len,
    x_hbm, w_hbm, rows_hbm, cols_hbm, scale_hbm, count_sm, table_hbm,
    out_ref,
    x_vm, tv_vm, w32_vm, w_vm, rows_sm, cols_sm, scale_sm, table_sm,
    rid_vm, cid_vm, wt_vm, row_send, col_send, part_vm,
    ready_sem, local_sem, x_send, x_row_sem, x_col_sem, p_send, p_row_sem, p_col_sem,
):
    me_row = lax.axis_index("row")
    me_col = lax.axis_index("col")
    blocks = piece_len // TILE
    chunk = piece_len * NVEC // LANES
    depth = slots * NVEC
    peers = n_row + n_col - 2
    row_x = x_vm.at[pl.ds(0, n_col)]
    col_x = x_vm.at[pl.ds(n_col, n_row)]

    def along_col(p):
        return (me_row, p)

    def along_row(p):
        return (p, me_col)

    def each(low, act):
        for me, total, place in ((me_col, n_col, along_col), (me_row, n_row, along_row)):
            for p in range(total):
                if (low and p < total - 1) or (not low and p > 0):
                    pl.when(p < me if low else p > me)(
                        functools.partial(act, p, place, place is along_col))

    barrier = pltpu.get_barrier_semaphore()

    def enter(p, place, is_col):
        pl.semaphore_signal(barrier, inc=1, device_id=place(p), device_id_type=MESH)

    def answer(p, place, is_col):
        pl.semaphore_signal(ready_sem, inc=1, device_id=place(p), device_id_type=MESH)

    def spread(p, place, is_col):
        slot = me_col if is_col else n_col + me_row
        pltpu.make_async_remote_copy(
            src_ref=x_hbm, dst_ref=x_vm.at[slot], send_sem=x_send,
            recv_sem=x_row_sem if is_col else x_col_sem,
            device_id=place(p), device_id_type=MESH).start()

    each(False, enter)
    lower = me_row + me_col

    @pl.when(lower > 0)
    def _():
        pl.semaphore_wait(barrier, lower)

    each(True, spread)
    each(True, answer)
    copies = [
        pltpu.make_async_copy(src, dst, local_sem.at[i])
        for i, (src, dst) in enumerate((
            (w_hbm, tv_vm),
            (rows_hbm, rows_sm),
            (cols_hbm, cols_sm),
            (scale_hbm, scale_sm),
            (table_hbm, table_sm),
        ))
    ]
    pltpu.make_async_copy(x_hbm, x_vm.at[me_col], x_row_sem).start()
    pltpu.make_async_copy(x_hbm, x_vm.at[n_col + me_row], x_col_sem).start()
    for copy in copies:
        copy.start()

    @pl.when(lower < peers)
    def _():
        pl.semaphore_wait(ready_sem, peers - lower)

    each(False, spread)

    copies[0].wait()
    relayout(slots, tv_vm, w32_vm, w_vm)
    for copy in copies[1:]:
        copy.wait()
    upper = lax.broadcasted_iota(jnp.int32, (8, LANES), 0) < NVEC
    for v in range(slots // 2):
        a, b = 2 * v, 2 * v + 1
        here = pl.ds(8 * v, 8)
        rid_vm[here, :] = jnp.where(upper, rows_sm[0, 0, a], rows_sm[0, 0, b])
        cid_vm[here, :] = jnp.where(upper, cols_sm[0, 0, a], cols_sm[0, 0, b])
        wt_vm[here, :] = jnp.where(
            upper, table_sm[scale_sm[0, 0, a]], table_sm[scale_sm[0, 0, b]])
    rid = rid_vm[...]
    cid = cid_vm[...]
    sub = lax.broadcasted_iota(jnp.int32, (depth, LANES), 0)
    lane = lax.broadcasted_iota(jnp.int32, (depth, LANES), 1)
    half = lax.div(lane, TILE)
    rid_piece, rid_block = lax.div(rid, blocks), lax.rem(rid, blocks)
    cid_piece, cid_block = lax.div(cid, blocks), lax.rem(cid, blocks)
    global_row = me_row * (n_col * blocks) + rid
    global_col = (cid_piece * n_col + me_col) * blocks + cid_block
    weight = jnp.where(global_row == global_col, 0.5, 1.0) * wt_vm[...]
    weight = jnp.where(lax.div(sub, NVEC) < count_sm[0, 0], weight, 0.0)

    def places(piece, block, total):
        target = piece * chunk + lax.div(block, 2) * NVEC + lax.rem(sub, NVEC)
        across = lax.broadcasted_iota(jnp.int32, (depth, total * chunk), 1)
        down = lax.broadcasted_iota(jnp.int32, (total * chunk, depth), 0)
        take = jnp.where(across == target[:, :1], 1.0, 0.0).astype(jnp.bfloat16)
        put = jnp.where(down == jnp.transpose(target)[:1, :], 1.0, 0.0).astype(jnp.bfloat16)
        return take, jnp.concatenate([put, put], axis=1), lax.rem(block, 2)

    take_row, put_row, odd_row = places(rid_piece, rid_block, n_col)
    take_col, put_col, odd_col = places(cid_piece, cid_block, n_row)
    row_weight = jnp.where(half == odd_row, weight, 0.0)
    col_weight = jnp.where(half == odd_col, weight, 0.0)

    def pick(take, pieces, odd):
        both = jnp.dot(take, pieces, preferred_element_type=jnp.float32)
        kept = jnp.where(half == odd, both, 0.0)
        return (kept + pltpu.roll(kept, TILE, 1)).astype(jnp.bfloat16)

    def place(put, values):
        high = values.astype(jnp.bfloat16)
        low = (values - high.astype(jnp.float32)).astype(jnp.bfloat16)
        return jnp.dot(
            put, jnp.concatenate([high, low], axis=0), preferred_element_type=jnp.float32)

    rows_of = GROUP * NVEC
    wide = GROUP * TILE
    g_row = lax.div(lax.broadcasted_iota(jnp.int32, (rows_of, wide), 0), NVEC)
    g_col = lax.div(lax.broadcasted_iota(jnp.int32, (rows_of, wide), 1), TILE)
    same = g_row == g_col

    def scatter(me, total, where, source, first, sem):
        for k in range(total - 1):
            p = k + jnp.where(me <= k, 1, 0)
            slot = first + lax.rem(me - p + total, total) - 1
            pltpu.make_async_remote_copy(
                src_ref=source.at[p], dst_ref=part_vm.at[slot], send_sem=p_send,
                recv_sem=sem, device_id=where(p), device_id_type=MESH).start()

    def forward():
        pltpu.make_async_copy(col_x, col_x, x_col_sem).wait()
        distant = pick(take_col, col_x[...].reshape(n_row * chunk, LANES), odd_col)
        parts = []
        for g in range(slots // GROUP):
            tiles = w_vm[g * wide:(g + 1) * wide, :]
            prod = lax.dot_general(
                distant[g * rows_of:(g + 1) * rows_of, :TILE], tiles[:, :TILE],
                (((1,), (1,)), ((), ())),
                preferred_element_type=jnp.float32)
            prod = jnp.where(same, prod, 0.0)
            total = prod[:, :LANES]
            for i in range(LANES, wide, LANES):
                total = total + prod[:, i:i + LANES]
            parts.append(total + pltpu.roll(total, TILE, 1))
        values = jnp.concatenate(parts, axis=0) * row_weight
        row_send[...] = place(put_row, values).reshape(n_col, chunk, LANES)
        scatter(me_col, n_col, along_col, row_send, 0, p_row_sem)

    def mirrored():
        pltpu.make_async_copy(row_x, row_x, x_row_sem).wait()
        near = pick(take_row, row_x[...].reshape(n_col * chunk, LANES), odd_row)
        parts = []
        for g in range(slots // GROUP):
            tiles = w_vm[g * wide:(g + 1) * wide, :]
            left = near[g * rows_of:(g + 1) * rows_of, :]
            left = jnp.concatenate([left] * (wide // LANES), axis=1)
            left = jnp.where(same, left, jnp.zeros_like(left))
            parts.append(jnp.dot(left, tiles, preferred_element_type=jnp.float32))
        values = jnp.concatenate(parts, axis=0) * col_weight
        col_send[...] = place(put_col, values).reshape(n_row, chunk, LANES)
        scatter(me_row, n_row, along_row, col_send, n_col - 1, p_col_sem)

    @pl.when(me_col == 0)
    def _():
        mirrored()
        forward()

    @pl.when(me_col > 0)
    def _():
        forward()
        mirrored()

    total = row_send[me_col] + col_send[me_row]
    got_row = part_vm.at[pl.ds(0, n_col - 1)]
    got_col = part_vm.at[pl.ds(n_col - 1, n_row - 1)]
    sent_x = x_vm.at[pl.ds(0, peers)]
    pltpu.make_async_copy(sent_x, sent_x, x_send).wait()
    pltpu.make_async_copy(got_row, got_row, p_row_sem).wait()
    for d in range(n_col - 1):
        total = total + part_vm[d]
    pltpu.make_async_copy(got_col, got_col, p_col_sem).wait()
    for d in range(n_col - 1, peers):
        total = total + part_vm[d]
    out_ref[...] = total
    pltpu.make_async_copy(part_vm, part_vm, p_send).wait()


def per_device(vectors, tile_values, tile_rows, tile_cols, tile_scale, tile_count, scale_table):
    n_row = lax.axis_size("row")
    n_col = lax.axis_size("col")
    piece_len = vectors.shape[1]
    slots = tile_rows.shape[-1]
    groups = piece_len // LANES
    chunk = groups * NVEC
    depth = slots * NVEC
    x = vectors.reshape(NVEC, groups, LANES).transpose(1, 0, 2).reshape(chunk, LANES)
    w = tile_values.reshape(slots, TILE * TILE)
    dma = pltpu.SemaphoreType.DMA
    hbm = pl.BlockSpec(memory_space=pltpu.HBM)
    out = pl.pallas_call(
        functools.partial(kernel, n_row, n_col, slots, piece_len),
        out_shape=pltpu.VMEM((chunk, LANES), jnp.float32),
        in_specs=[hbm] * 5 + [pl.BlockSpec(memory_space=pltpu.SMEM), hbm],
        out_specs=pl.BlockSpec(memory_space=pltpu.VMEM),
        scratch_shapes=[
            pltpu.VMEM((n_col + n_row, chunk, LANES), jnp.bfloat16),
            pltpu.VMEM((slots, TILE * TILE), jnp.bfloat16),
            pltpu.VMEM((slots, TILE, LANES), jnp.float32),
            pltpu.VMEM((slots * TILE, LANES), jnp.bfloat16),
            pltpu.SMEM(tile_rows.shape, jnp.int32),
            pltpu.SMEM(tile_cols.shape, jnp.int32),
            pltpu.SMEM(tile_scale.shape, jnp.int32),
            pltpu.SMEM(scale_table.shape, jnp.float32),
            pltpu.VMEM((depth, LANES), jnp.int32),
            pltpu.VMEM((depth, LANES), jnp.int32),
            pltpu.VMEM((depth, LANES), jnp.float32),
            pltpu.VMEM((n_col, chunk, LANES), jnp.float32),
            pltpu.VMEM((n_row, chunk, LANES), jnp.float32),
            pltpu.VMEM((n_col + n_row - 2, chunk, LANES), jnp.float32),
            pltpu.SemaphoreType.REGULAR,
            dma((5,)), dma, dma, dma, dma, dma, dma,
        ],
        compiler_params=pltpu.CompilerParams(collective_id=0, has_side_effects=True),
        name="lanczos",
    )(x, w, tile_rows, tile_cols, tile_scale, tile_count, scale_table)
    return out.reshape(groups, NVEC, LANES).transpose(1, 0, 2).reshape(NVEC, piece_len)


def solution(mesh):
    return jax.shard_map(
        per_device,
        mesh=mesh,
        in_specs=(
            P(None, ("row", "col")),
            P("row", "col", None, None),
            P("row", "col", None),
            P("row", "col", None),
            P("row", "col", None),
            P("row", "col"),
            P(),
        ),
        out_specs=P(None, ("row", "col")),
        check_vma=False,
    )
```

```python
import functools

import jax
import jax.numpy as jnp
from jax import lax
from jax.experimental import pallas as pl
from jax.experimental.pallas import tpu as pltpu
from jax.sharding import PartitionSpec as P

TILE = 64
NVEC = 4
LANES = 128
GROUP = 4
MESH = pl.DeviceIdType.MESH


def relayout(slots, tv_vm, w32_vm, w_vm):
    pack = LANES // TILE
    step = max(1, 2 * LANES // (pack * slots))
    depth = pack * step * slots
    r = lax.broadcasted_iota(jnp.int32, (depth, depth), 0)
    c = lax.broadcasted_iota(jnp.int32, (depth, depth), 1)
    slot, i = lax.div(r, pack * step), lax.rem(r, pack * step)
    source = (lax.rem(i, pack) * step + lax.div(i, pack)) * slots + slot
    order = jnp.where(c == source, 1.0, 0.0).astype(jnp.bfloat16)
    low_half = lax.broadcasted_iota(jnp.int32, (slots, LANES), 1) < TILE
    total = TILE * TILE // LANES
    for first in range(0, total, step):
        low, high = [], []
        for g in range(first, first + step):
            part = tv_vm[:, g * LANES:(g + 1) * LANES].astype(jnp.float32)
            turned = pltpu.roll(part, TILE, 1)
            low.append(jnp.where(low_half, part, turned).astype(jnp.bfloat16))
            high.append(jnp.where(low_half, turned, part).astype(jnp.bfloat16))
        moved = jnp.dot(
            order, jnp.concatenate(low + high, axis=0), preferred_element_type=jnp.float32)
        w32_vm[:, first * pack:(first + step) * pack, :] = moved.reshape(
            slots, pack * step, LANES)
    w_vm[...] = w32_vm[...].reshape(slots * TILE, LANES).astype(jnp.bfloat16)


def kernel(
    n_row, n_col, slots, piece_len,
    x_hbm, w_hbm, rows_hbm, cols_hbm, scale_hbm, count_sm, table_hbm,
    out_ref,
    x_vm, tv_vm, w32_vm, w_vm, index_sm, table_sm,
    rid_vm, cid_vm, wt_vm, row_send, col_send, part_vm,
    ready_sem, own_sem, tile_sem, index_sem, table_sem,
    x_send, x_row_sem, x_col_sem, p_send, p_row_sem, p_col_sem,
):
    me_row = lax.axis_index("row")
    me_col = lax.axis_index("col")
    blocks = piece_len // TILE
    chunk = piece_len * NVEC // LANES
    depth = slots * NVEC
    peers = n_row + n_col - 2
    row_x = x_vm.at[pl.ds(0, n_col)]
    col_x = x_vm.at[pl.ds(n_col, n_row)]

    def along_col(p):
        return (me_row, p)

    def along_row(p):
        return (p, me_col)

    def each(low, act):
        for me, total, place in ((me_col, n_col, along_col), (me_row, n_row, along_row)):
            for p in range(total):
                if (low and p < total - 1) or (not low and p > 0):
                    pl.when(p < me if low else p > me)(
                        functools.partial(act, p, place, place is along_col))

    barrier = pltpu.get_barrier_semaphore()

    def enter(p, place, is_col):
        pl.semaphore_signal(barrier, inc=1, device_id=place(p), device_id_type=MESH)

    def answer(p, place, is_col):
        pl.semaphore_signal(ready_sem, inc=1, device_id=place(p), device_id_type=MESH)

    def spread(p, place, is_col):
        slot = me_col if is_col else n_col + me_row
        pltpu.make_async_remote_copy(
            src_ref=x_vm.at[me_col], dst_ref=x_vm.at[slot], send_sem=x_send,
            recv_sem=x_row_sem if is_col else x_col_sem,
            device_id=place(p), device_id_type=MESH).start()

    own = pltpu.make_async_copy(x_hbm, x_vm.at[me_col], own_sem)
    again = pltpu.make_async_copy(x_hbm, x_vm.at[n_col + me_row], x_col_sem)
    tiles_in = pltpu.make_async_copy(w_hbm, tv_vm, tile_sem)
    table_in = pltpu.make_async_copy(table_hbm, table_sm, table_sem)
    own.start()
    each(False, enter)
    again.start()
    tiles_in.start()
    for i, src in enumerate((rows_hbm, cols_hbm, scale_hbm)):
        pltpu.make_async_copy(src, index_sm.at[i], index_sem).start()
    table_in.start()
    own.wait()
    lower = me_row + me_col

    @pl.when(lower > 0)
    def _():
        pl.semaphore_wait(barrier, lower)

    each(True, spread)
    each(True, answer)

    @pl.when(lower < peers)
    def _():
        pl.semaphore_wait(ready_sem, peers - lower)

    each(False, spread)

    tiles_in.wait()
    relayout(slots, tv_vm, w32_vm, w_vm)
    pltpu.make_async_copy(index_sm, index_sm, index_sem).wait()
    table_in.wait()
    upper = lax.broadcasted_iota(jnp.int32, (8, LANES), 0) < NVEC
    for v in range(slots // 2):
        a, b = 2 * v, 2 * v + 1
        here = pl.ds(8 * v, 8)
        rid_vm[here, :] = jnp.where(upper, index_sm[0, 0, 0, a], index_sm[0, 0, 0, b])
        cid_vm[here, :] = jnp.where(upper, index_sm[1, 0, 0, a], index_sm[1, 0, 0, b])
        wt_vm[here, :] = jnp.where(
            upper, table_sm[index_sm[2, 0, 0, a]], table_sm[index_sm[2, 0, 0, b]])
    rid = rid_vm[...]
    cid = cid_vm[...]
    sub = lax.broadcasted_iota(jnp.int32, (depth, LANES), 0)
    lane = lax.broadcasted_iota(jnp.int32, (depth, LANES), 1)
    half = lax.div(lane, TILE)
    rid_piece, rid_block = lax.div(rid, blocks), lax.rem(rid, blocks)
    cid_piece, cid_block = lax.div(cid, blocks), lax.rem(cid, blocks)
    global_row = me_row * (n_col * blocks) + rid
    global_col = (cid_piece * n_col + me_col) * blocks + cid_block
    weight = jnp.where(global_row == global_col, 0.5, 1.0) * wt_vm[...]
    weight = jnp.where(lax.div(sub, NVEC) < count_sm[0, 0], weight, 0.0)

    def places(piece, block, total):
        target = piece * chunk + lax.div(block, 2) * NVEC + lax.rem(sub, NVEC)
        across = lax.broadcasted_iota(jnp.int32, (depth, total * chunk), 1)
        down = lax.broadcasted_iota(jnp.int32, (total * chunk, depth), 0)
        take = jnp.where(across == target[:, :1], 1.0, 0.0).astype(jnp.bfloat16)
        put = jnp.where(down == jnp.transpose(target)[:1, :], 1.0, 0.0).astype(jnp.bfloat16)
        return take, jnp.concatenate([put, put], axis=1), lax.rem(block, 2)

    take_row, put_row, odd_row = places(rid_piece, rid_block, n_col)
    take_col, put_col, odd_col = places(cid_piece, cid_block, n_row)
    row_weight = jnp.where(half == odd_row, weight, 0.0)
    col_weight = jnp.where(half == odd_col, weight, 0.0)

    def pick(take, pieces, odd):
        both = jnp.dot(take, pieces, preferred_element_type=jnp.float32)
        kept = jnp.where(half == odd, both, 0.0)
        return (kept + pltpu.roll(kept, TILE, 1)).astype(jnp.bfloat16)

    def place(put, values):
        high = values.astype(jnp.bfloat16)
        low = (values - high.astype(jnp.float32)).astype(jnp.bfloat16)
        return jnp.dot(
            put, jnp.concatenate([high, low], axis=0), preferred_element_type=jnp.float32)

    rows_of = GROUP * NVEC
    wide = GROUP * TILE
    g_row = lax.div(lax.broadcasted_iota(jnp.int32, (rows_of, wide), 0), NVEC)
    g_col = lax.div(lax.broadcasted_iota(jnp.int32, (rows_of, wide), 1), TILE)
    same = g_row == g_col

    def scatter(me, total, where, source, first, sem):
        for k in range(total - 1):
            p = k + jnp.where(me <= k, 1, 0)
            slot = first + lax.rem(me - p + total, total) - 1
            pltpu.make_async_remote_copy(
                src_ref=source.at[p], dst_ref=part_vm.at[slot], send_sem=p_send,
                recv_sem=sem, device_id=where(p), device_id_type=MESH).start()

    def forward():
        pltpu.make_async_copy(col_x, col_x, x_col_sem).wait()
        distant = pick(take_col, col_x[...].reshape(n_row * chunk, LANES), odd_col)
        parts = []
        for g in range(slots // GROUP):
            tiles = w_vm[g * wide:(g + 1) * wide, :]
            prod = lax.dot_general(
                distant[g * rows_of:(g + 1) * rows_of, :TILE], tiles[:, :TILE],
                (((1,), (1,)), ((), ())),
                preferred_element_type=jnp.float32)
            prod = jnp.where(same, prod, 0.0)
            total = prod[:, :LANES]
            for i in range(LANES, wide, LANES):
                total = total + prod[:, i:i + LANES]
            parts.append(total + pltpu.roll(total, TILE, 1))
        values = jnp.concatenate(parts, axis=0) * row_weight
        row_send[...] = place(put_row, values).reshape(n_col, chunk, LANES)
        scatter(me_col, n_col, along_col, row_send, 0, p_row_sem)

    def mirrored():
        others = row_x.at[pl.ds(0, n_col - 1)]
        pltpu.make_async_copy(others, others, x_row_sem).wait()
        near = pick(take_row, row_x[...].reshape(n_col * chunk, LANES), odd_row)
        parts = []
        for g in range(slots // GROUP):
            tiles = w_vm[g * wide:(g + 1) * wide, :]
            left = near[g * rows_of:(g + 1) * rows_of, :]
            left = jnp.concatenate([left] * (wide // LANES), axis=1)
            left = jnp.where(same, left, jnp.zeros_like(left))
            parts.append(jnp.dot(left, tiles, preferred_element_type=jnp.float32))
        values = jnp.concatenate(parts, axis=0) * col_weight
        col_send[...] = place(put_col, values).reshape(n_row, chunk, LANES)
        scatter(me_row, n_row, along_row, col_send, n_col - 1, p_col_sem)

    @pl.when(me_col == 0)
    def _():
        mirrored()
        forward()

    @pl.when(me_col > 0)
    def _():
        forward()
        mirrored()

    total = row_send[me_col] + col_send[me_row]
    got_row = part_vm.at[pl.ds(0, n_col - 1)]
    got_col = part_vm.at[pl.ds(n_col - 1, n_row - 1)]
    sent_x = x_vm.at[pl.ds(0, peers)]
    pltpu.make_async_copy(sent_x, sent_x, x_send).wait()
    pltpu.make_async_copy(got_row, got_row, p_row_sem).wait()
    for d in range(n_col - 1):
        total = total + part_vm[d]
    pltpu.make_async_copy(got_col, got_col, p_col_sem).wait()
    for d in range(n_col - 1, peers):
        total = total + part_vm[d]
    out_ref[...] = total
    pltpu.make_async_copy(part_vm, part_vm, p_send).wait()


def per_device(vectors, tile_values, tile_rows, tile_cols, tile_scale, tile_count, scale_table):
    n_row = lax.axis_size("row")
    n_col = lax.axis_size("col")
    piece_len = vectors.shape[1]
    slots = tile_rows.shape[-1]
    groups = piece_len // LANES
    chunk = groups * NVEC
    depth = slots * NVEC
    x = vectors.reshape(NVEC, groups, LANES).transpose(1, 0, 2).reshape(chunk, LANES)
    w = tile_values.reshape(slots, TILE * TILE)
    dma = pltpu.SemaphoreType.DMA
    hbm = pl.BlockSpec(memory_space=pltpu.HBM)
    out = pl.pallas_call(
        functools.partial(kernel, n_row, n_col, slots, piece_len),
        out_shape=pltpu.VMEM((chunk, LANES), jnp.float32),
        in_specs=[hbm] * 5 + [pl.BlockSpec(memory_space=pltpu.SMEM), hbm],
        out_specs=pl.BlockSpec(memory_space=pltpu.VMEM),
        scratch_shapes=[
            pltpu.VMEM((n_col + n_row, chunk, LANES), jnp.bfloat16),
            pltpu.VMEM((slots, TILE * TILE), jnp.bfloat16),
            pltpu.VMEM((slots, TILE, LANES), jnp.float32),
            pltpu.VMEM((slots * TILE, LANES), jnp.bfloat16),
            pltpu.SMEM((3,) + tile_rows.shape, jnp.int32),
            pltpu.SMEM(scale_table.shape, jnp.float32),
            pltpu.VMEM((depth, LANES), jnp.int32),
            pltpu.VMEM((depth, LANES), jnp.int32),
            pltpu.VMEM((depth, LANES), jnp.float32),
            pltpu.VMEM((n_col, chunk, LANES), jnp.float32),
            pltpu.VMEM((n_row, chunk, LANES), jnp.float32),
            pltpu.VMEM((n_col + n_row - 2, chunk, LANES), jnp.float32),
            pltpu.SemaphoreType.REGULAR,
            dma, dma, dma, dma, dma, dma, dma, dma, dma, dma,
        ],
        compiler_params=pltpu.CompilerParams(collective_id=0, has_side_effects=True),
        name="lanczos",
    )(x, w, tile_rows, tile_cols, tile_scale, tile_count, scale_table)
    return out.reshape(groups, NVEC, LANES).transpose(1, 0, 2).reshape(NVEC, piece_len)


def solution(mesh):
    return jax.shard_map(
        per_device,
        mesh=mesh,
        in_specs=(
            P(None, ("row", "col")),
            P("row", "col", None, None),
            P("row", "col", None),
            P("row", "col", None),
            P("row", "col", None),
            P("row", "col"),
            P(),
        ),
        out_specs=P(None, ("row", "col")),
        check_vma=False,
    )
```

```python
import functools

import jax
import jax.numpy as jnp
from jax import lax
from jax.experimental import pallas as pl
from jax.experimental.pallas import tpu as pltpu
from jax.sharding import PartitionSpec as P

TILE = 64
NVEC = 4
LANES = 128
MESH = pl.DeviceIdType.MESH


def relayout(slots, tv_vm, w_vm):
    across = slots // 2
    pack = LANES // TILE
    step = max(1, 2 * LANES // (pack * across))
    depth = pack * step * across
    r = lax.broadcasted_iota(jnp.int32, (depth, depth), 0)
    c = lax.broadcasted_iota(jnp.int32, (depth, depth), 1)
    slot, i = lax.div(r, pack * step), lax.rem(r, pack * step)
    source = (lax.rem(i, pack) * step + lax.div(i, pack)) * across + slot
    order = jnp.where(c == source, 1.0, 0.0).astype(jnp.bfloat16)
    low_half = lax.broadcasted_iota(jnp.int32, (across, LANES), 1) < TILE
    total = TILE * TILE // LANES
    for first in range(0, total, step):
        even, odd = [], []
        for g in range(first, first + step):
            part = tv_vm[:, g * LANES:(g + 1) * LANES].astype(jnp.float32)
            turned = pltpu.roll(part, TILE, 1)
            even.append(jnp.where(low_half, part[:across], turned[across:]).astype(jnp.bfloat16))
            odd.append(jnp.where(low_half, turned[:across], part[across:]).astype(jnp.bfloat16))
        moved = jnp.dot(
            order, jnp.concatenate(even + odd, axis=0), preferred_element_type=jnp.float32)
        w_vm[:, first * pack:(first + step) * pack, :] = moved.reshape(
            across, pack * step, LANES).astype(jnp.bfloat16)


def kernel(
    n_row, n_col, slots, piece_len,
    x_hbm, w_hbm, rows_hbm, cols_hbm, scale_hbm, count_sm, table_hbm,
    out_ref,
    near_vm, far_vm, tv_vm, w_vm, index_sm, table_sm, spot_sm,
    rid_vm, cid_vm, wt_vm, pick_vm, row_send, col_send, part_vm,
    ready_sem, own_sem, index_sem, table_sem, x_send, x_row_sem, x_col_sem, p_send, p_sem,
):
    me_row = lax.axis_index("row")
    me_col = lax.axis_index("col")
    blocks = piece_len // TILE
    chunk = piece_len * NVEC // LANES
    depth = slots * NVEC
    peers = n_row + n_col - 2
    groups = piece_len // LANES

    def piece(ref, slot):
        return ref.at[pl.ds(slot * groups, groups)]

    def arrived(ref, sem):
        pltpu.make_async_copy(ref, ref, sem).wait()

    def along_col(p):
        return (me_row, p)

    def along_row(p):
        return (p, me_col)

    quarter = n_row // 4

    def between(place, n):
        return jnp.where(lax.div(place, quarter) == n, 1, 0)

    def each(low, greet, act):
        cols = [(p, me_col, n_col, along_col) for p in range(n_col)]
        rows = [(p, me_row, n_row, along_row) for p in range(n_row)]
        if not low:
            cols, rows = cols[::-1], rows[::-1]
        for p, me, total, where in cols[:1] + rows[:1] + cols[1:2] + rows[1:] + cols[2:]:
            if (low and p == total - 1) or (not low and p == 0):
                continue
            meets = p < me if low else p > me
            level = p // quarter
            if where is along_row and level in (1, 2):
                unlike = lax.div(me, quarter) != 3 - level
                apart = jnp.logical_and(meets, unlike)
                late = jnp.logical_or(meets, lax.div(me, quarter) == 3 - level)
                meets = apart if low or greet else late
            pl.when(meets)(functools.partial(act, p, where, where is along_col))

    barrier = pltpu.get_barrier_semaphore()

    def enter(p, place, is_col):
        pl.semaphore_signal(barrier, inc=1, device_id=place(p), device_id_type=MESH)

    def answer(p, place, is_col):
        pl.semaphore_signal(ready_sem, inc=1, device_id=place(p), device_id_type=MESH)

    def spread(p, place, is_col):
        pltpu.make_async_remote_copy(
            src_ref=piece(near_vm, me_col),
            dst_ref=piece(near_vm, me_col) if is_col else piece(far_vm, me_row), send_sem=x_send,
            recv_sem=x_row_sem if is_col else x_col_sem,
            device_id=place(p), device_id_type=MESH).start()

    own = pltpu.make_async_copy(x_hbm, piece(near_vm, me_col), own_sem)
    again = pltpu.make_async_copy(x_hbm, piece(far_vm, me_row), x_col_sem)
    tiles_in = pltpu.make_async_copy(w_hbm, tv_vm, own_sem)
    table_in = pltpu.make_async_copy(table_hbm, table_sm, table_sem)
    own.start()
    each(False, True, enter)
    again.start()
    for i, src in enumerate((rows_hbm, cols_hbm, scale_hbm)):
        pltpu.make_async_copy(src, index_sm.at[i], index_sem).start()
    table_in.start()
    lower = me_row + me_col - quarter * between(me_row, 2)
    higher = peers - me_row - me_col - quarter * between(me_row, 1)

    @pl.when(lower > 0)
    def _():
        pl.semaphore_wait(barrier, lower)

    each(True, True, answer)
    own.wait()
    tiles_in.start()
    each(True, False, spread)

    @pl.when(higher > 0)
    def _():
        pl.semaphore_wait(ready_sem, higher)

    each(False, False, spread)

    tiles_in.wait()
    relayout(slots, tv_vm, w_vm)
    arrived(index_sm, index_sem)
    table_in.wait()
    for t in range(slots):
        spot_sm[0, t] = lax.shift_right_logical(index_sm[0, 0, 0, t], 1)
        spot_sm[1, t] = lax.shift_right_logical(index_sm[1, 0, 0, t], 1)
    upper = lax.broadcasted_iota(jnp.int32, (8, LANES), 0) < NVEC
    for v in range(slots // 2):
        a, b = 2 * v, 2 * v + 1
        here = pl.ds(8 * v, 8)
        rid_vm[here, :] = jnp.where(upper, index_sm[0, 0, 0, a], index_sm[0, 0, 0, b])
        cid_vm[here, :] = jnp.where(upper, index_sm[1, 0, 0, a], index_sm[1, 0, 0, b])
        wt_vm[here, :] = jnp.where(
            upper, table_sm[index_sm[2, 0, 0, a]], table_sm[index_sm[2, 0, 0, b]])
    rid = rid_vm[...]
    cid = cid_vm[...]
    sub = lax.broadcasted_iota(jnp.int32, (depth, LANES), 0)
    lane = lax.broadcasted_iota(jnp.int32, (depth, LANES), 1)
    half = lax.div(lane, TILE)
    cid_piece, cid_block = lax.div(cid, blocks), lax.rem(cid, blocks)
    global_row = me_row * (n_col * blocks) + rid
    global_col = (cid_piece * n_col + me_col) * blocks + cid_block
    weight = jnp.where(global_row == global_col, 0.5, 1.0) * wt_vm[...]
    weight = jnp.where(lax.div(sub, NVEC) < count_sm[0, 0], weight, 0.0)

    pair = 2 * NVEC
    first = lax.div(sub, depth // 2)
    second = lax.rem(lax.div(sub, NVEC), 2)

    def turn(values):
        return jnp.concatenate([
            pltpu.roll(values[v * pair:(v + 1) * pair], NVEC, 0)
            for v in range(slots // 2)], axis=0)

    def places(block):
        spot = lax.div(block, 2)
        line, part = lax.div(spot, 2), lax.rem(spot, 2)
        stay = jnp.where(part == second, line, -1)
        move = turn(jnp.where(part != second, line, -1))
        return stay, move, lax.rem(block, 2)

    stay_row, move_row, odd_row = places(rid)
    stay_col, move_col, odd_col = places(cid)
    row_weight = jnp.where(half == odd_row, weight, 0.0)
    col_weight = jnp.where(half == odd_col, weight, 0.0)

    def pick(x_vm, which, odd, want):
        for t in range(slots):
            pick_vm[t * NVEC:(t + 1) * NVEC, :] = x_vm[spot_sm[which, t]].astype(jnp.float32)
        both = pick_vm[...]
        moved = jnp.where(odd == want, both, pltpu.roll(both, TILE, 1))
        return jnp.where(half == want, moved, 0.0)

    def finish(values, odd, have, weights):
        return jnp.where(odd == have, values, pltpu.roll(values, TILE, 1)) * weights

    def place(k, stay, move, values, turned):
        lines = []
        for n in range(chunk // pair):
            line = k * (chunk // pair) + n
            terms = [
                jnp.where(at[v * pair:(v + 1) * pair] == line, of[v * pair:(v + 1) * pair], 0.0)
                for v in range(slots // 2) for at, of in ((stay, values), (move, turned))]
            while len(terms) > 1:
                terms = [sum(terms[i + 1:i + 2], terms[i]) for i in range(0, len(terms), 2)]
            lines.append(terms[0])
        return jnp.concatenate(lines, axis=0)

    sets = slots // 16
    blank = jnp.zeros((2 * pair, LANES), jnp.bfloat16)

    def at(b0, m, b1, a1):
        return ((b0 * sets + m) * 2 + b1) * 2 + a1

    def left(rows, spots):
        def two(group):
            return jnp.concatenate(
                [rows[v * pair:(v + 1) * pair] for v in group], axis=0).astype(jnp.bfloat16)
        return jnp.concatenate([
            jnp.concatenate([two(spots[0]), blank], axis=1),
            jnp.concatenate([blank, two(spots[1])], axis=1)], axis=0)

    def tiles(m):
        return jnp.concatenate([
            w_vm[(m * 2 + b1) * 4:(m * 2 + b1) * 4 + 4].reshape(4 * TILE, LANES)
            for b1 in range(2)], axis=1)

    def collect(found, spots, result):
        for n, v in enumerate(spots[0] + spots[1]):
            found[v] = result[n * pair:(n + 1) * pair]

    def scatter(me, total, where, source, first, sem, stay, move, values):
        turned = turn(values)
        for k in range(total):
            source[k] = place(k, stay, move, values, turned)

            @pl.when(me != k)
            def _():
                slot = first + lax.rem(me - k + total, total) - 1
                pltpu.make_async_remote_copy(
                    src_ref=source.at[k], dst_ref=part_vm.at[slot], send_sem=p_send,
                    recv_sem=sem, device_id=where(k), device_id_type=MESH).start()

    def forward():
        arrived(far_vm, x_col_sem)
        distant = pick(far_vm, 1, odd_col, first)
        found = [None] * (slots // 2)
        for m in range(sets):
            spots = [[[at(b0, m, b1, a1) for b0 in range(2)] for b1 in range(2)]
                     for a1 in range(2)]
            result = lax.dot_general(
                jnp.concatenate([left(distant, spots[0]), left(distant, spots[1])], axis=0),
                tiles(m), (((1,), (1,)), ((), ())), preferred_element_type=jnp.float32)
            for a1 in range(2):
                collect(found, spots[a1], result[
                    a1 * 4 * pair:(a1 + 1) * 4 * pair, a1 * LANES:(a1 + 1) * LANES])
        values = finish(jnp.concatenate(found, axis=0), odd_row, second, row_weight)
        scatter(me_col, n_col, along_col, row_send, 0, p_sem, stay_row, move_row, values)

    def mirrored():
        arrived(near_vm.at[pl.ds(0, (n_col - 1) * groups)], x_row_sem)
        near = pick(near_vm, 0, odd_row, second)
        found = [None] * (slots // 2)
        for m in range(sets):
            spots = [[[at(b0, m, b1, a1) for b0 in range(2)] for a1 in range(2)]
                     for b1 in range(2)]
            result = jnp.dot(
                jnp.concatenate([left(near, spots[0]), left(near, spots[1])], axis=0),
                tiles(m), preferred_element_type=jnp.float32)
            for b1 in range(2):
                collect(found, spots[b1], result[
                    b1 * 4 * pair:(b1 + 1) * 4 * pair, b1 * LANES:(b1 + 1) * LANES])
        values = finish(jnp.concatenate(found, axis=0), odd_col, first, col_weight)
        scatter(
            me_row, n_row, along_row, col_send, n_col - 1, p_sem, stay_col, move_col, values)

    @pl.when(me_col == 0)
    def _():
        mirrored()
        forward()

    @pl.when(me_col > 0)
    def _():
        forward()
        mirrored()

    total = row_send[me_col] + col_send[me_row]
    arrived(part_vm.at[pl.ds(0, peers // 2)], x_send)
    arrived(part_vm, p_sem)
    for d in range(peers):
        total = total + part_vm[d]
    out_ref[...] = total
    arrived(part_vm, p_send)


def per_device(vectors, tile_values, tile_rows, tile_cols, tile_scale, tile_count, scale_table):
    n_row = lax.axis_size("row")
    n_col = lax.axis_size("col")
    piece_len = vectors.shape[1]
    slots = tile_rows.shape[-1]
    groups = piece_len // LANES
    chunk = groups * NVEC
    depth = slots * NVEC
    x = vectors.reshape(NVEC, groups, LANES).transpose(1, 0, 2)
    w = tile_values.reshape(slots, TILE * TILE)
    dma = pltpu.SemaphoreType.DMA
    hbm = pl.BlockSpec(memory_space=pltpu.HBM)
    out = pl.pallas_call(
        functools.partial(kernel, n_row, n_col, slots, piece_len),
        out_shape=pltpu.VMEM((chunk, LANES), jnp.float32),
        in_specs=[hbm] * 5 + [pl.BlockSpec(memory_space=pltpu.SMEM), hbm],
        out_specs=pl.BlockSpec(memory_space=pltpu.VMEM),
        scratch_shapes=[
            pltpu.VMEM((n_col * groups, NVEC, LANES), jnp.bfloat16),
            pltpu.VMEM((n_row * groups, NVEC, LANES), jnp.bfloat16),
            pltpu.VMEM((slots, TILE * TILE), jnp.bfloat16),
            pltpu.VMEM((slots // 2, TILE, LANES), jnp.bfloat16),
            pltpu.SMEM((3,) + tile_rows.shape, jnp.int32),
            pltpu.SMEM(scale_table.shape, jnp.float32),
            pltpu.SMEM((2, slots), jnp.int32),
            pltpu.VMEM((depth, LANES), jnp.int32),
            pltpu.VMEM((depth, LANES), jnp.int32),
            pltpu.VMEM((depth, LANES), jnp.float32),
            pltpu.VMEM((depth, LANES), jnp.float32),
            pltpu.VMEM((n_col, chunk, LANES), jnp.float32),
            pltpu.VMEM((n_row, chunk, LANES), jnp.float32),
            pltpu.VMEM((n_col + n_row - 2, chunk, LANES), jnp.float32),
            pltpu.SemaphoreType.REGULAR, dma, dma, dma, dma, dma, dma, dma, dma,
        ],
        compiler_params=pltpu.CompilerParams(collective_id=0, has_side_effects=True),
        name="lanczos",
    )(x, w, tile_rows, tile_cols, tile_scale, tile_count, scale_table)
    return out.reshape(groups, NVEC, LANES).transpose(1, 0, 2).reshape(NVEC, piece_len)


def solution(mesh):
    return jax.shard_map(
        per_device,
        mesh=mesh,
        in_specs=(
            P(None, ("row", "col")),
            P("row", "col", None, None),
            P("row", "col", None),
            P("row", "col", None),
            P("row", "col", None),
            P("row", "col"),
            P(),
        ),
        out_specs=P(None, ("row", "col")),
        check_vma=False,
    )
```

```python
import functools

import jax
import jax.numpy as jnp
from jax import lax
from jax.experimental import pallas as pl
from jax.experimental.pallas import tpu as pltpu
from jax.sharding import PartitionSpec as P

TILE = 64
NVEC = 4
LANES = 128
MESH = pl.DeviceIdType.MESH


def relayout(slots, tv_vm, w_vm):
    across = slots // 2
    pack = LANES // TILE
    step = max(1, 2 * LANES // (pack * across))
    depth = pack * step * across
    r = lax.broadcasted_iota(jnp.int32, (depth, depth), 0)
    c = lax.broadcasted_iota(jnp.int32, (depth, depth), 1)
    slot, i = lax.div(r, pack * step), lax.rem(r, pack * step)
    source = (lax.rem(i, pack) * step + lax.div(i, pack)) * across + slot
    order = jnp.where(c == source, 1.0, 0.0).astype(jnp.bfloat16)
    low_half = lax.broadcasted_iota(jnp.int32, (across, LANES), 1) < TILE
    total = TILE * TILE // LANES
    for first in range(0, total, step):
        even, odd = [], []
        for g in range(first, first + step):
            part = tv_vm[:, g * LANES:(g + 1) * LANES].astype(jnp.float32)
            turned = pltpu.roll(part, TILE, 1)
            even.append(jnp.where(low_half, part[:across], turned[across:]).astype(jnp.bfloat16))
            odd.append(jnp.where(low_half, turned[:across], part[across:]).astype(jnp.bfloat16))
        moved = jnp.dot(
            order, jnp.concatenate(even + odd, axis=0), preferred_element_type=jnp.float32)
        w_vm[:, first * pack:(first + step) * pack, :] = moved.reshape(
            across, pack * step, LANES).astype(jnp.bfloat16)


def kernel(
    n_row, n_col, slots, piece_len,
    x_hbm, w_hbm, rows_hbm, cols_hbm, scale_hbm, count_sm, table_hbm,
    out_ref,
    near_vm, far_vm, tv_vm, w_vm, index_sm, table_sm, spot_sm,
    rid_vm, cid_vm, wt_vm, pick_vm, row_send, col_send, part_vm,
    ready_sem, own_sem, index_sem, send_sem, x_row_sem, x_col_sem, p_sem,
):
    me_row = lax.axis_index("row")
    me_col = lax.axis_index("col")
    blocks = piece_len // TILE
    chunk = piece_len * NVEC // LANES
    depth = slots * NVEC
    peers = n_row + n_col - 2
    groups = piece_len // LANES

    def piece(ref, slot):
        return ref.at[pl.ds(slot * groups, groups)]

    def arrived(ref, sem):
        pltpu.make_async_copy(ref, ref, sem).wait()

    def along_col(p):
        return (me_row, p)

    def along_row(p):
        return (p, me_col)

    quarter = n_row // 4

    def between(place, n):
        return jnp.where(lax.div(place, quarter) == n, 1, 0)

    def each(low, greet, act):
        cols = [(p, me_col, n_col, along_col) for p in range(n_col)]
        rows = [(p, me_row, n_row, along_row) for p in range(n_row)]
        if not low:
            cols, rows = cols[::-1], rows[::-1]
        for p, me, total, where in cols[:1] + rows[:1] + cols[1:2] + rows[1:] + cols[2:]:
            if (low and p == total - 1) or (not low and p == 0):
                continue
            meets = p < me if low else p > me
            level = p // quarter
            if where is along_row and level in (1, 2):
                unlike = lax.div(me, quarter) != 3 - level
                apart = jnp.logical_and(meets, unlike)
                late = jnp.logical_or(meets, lax.div(me, quarter) == 3 - level)
                meets = apart if low or greet else late
            pl.when(meets)(functools.partial(act, p, where, where is along_col))

    barrier = pltpu.get_barrier_semaphore()

    def enter(p, place, is_col):
        pl.semaphore_signal(barrier, inc=1, device_id=place(p), device_id_type=MESH)

    def answer(p, place, is_col):
        pl.semaphore_signal(ready_sem, inc=1, device_id=place(p), device_id_type=MESH)

    def spread(p, place, is_col):
        pltpu.make_async_remote_copy(
            src_ref=piece(near_vm, me_col),
            dst_ref=piece(near_vm, me_col) if is_col else piece(far_vm, me_row), send_sem=send_sem,
            recv_sem=x_row_sem if is_col else x_col_sem,
            device_id=place(p), device_id_type=MESH).start()

    own = pltpu.make_async_copy(x_hbm, piece(near_vm, me_col), own_sem)
    again = pltpu.make_async_copy(x_hbm, piece(far_vm, me_row), x_col_sem)
    tiles_in = pltpu.make_async_copy(w_hbm, tv_vm, own_sem)
    table_in = pltpu.make_async_copy(table_hbm, table_sm, index_sem)
    own.start()
    each(False, True, enter)
    again.start()
    for i, src in enumerate((rows_hbm, cols_hbm, scale_hbm)):
        pltpu.make_async_copy(src, index_sm.at[i], index_sem).start()
    lower = me_row + me_col - quarter * between(me_row, 2)
    higher = peers - me_row - me_col - quarter * between(me_row, 1)

    @pl.when(lower > 0)
    def _():
        pl.semaphore_wait(barrier, lower)

    each(True, True, answer)
    own.wait()
    each(True, False, spread)
    tiles_in.start()
    arrived(index_sm, index_sem)
    table_in.start()

    @pl.when(higher > 0)
    def _():
        pl.semaphore_wait(ready_sem, higher)

    each(False, False, spread)

    tiles_in.wait()
    relayout(slots, tv_vm, w_vm)
    table_in.wait()
    for t in range(slots):
        spot_sm[0, t] = lax.shift_right_logical(index_sm[0, 0, 0, t], 1)
        spot_sm[1, t] = lax.shift_right_logical(index_sm[1, 0, 0, t], 1)
    upper = lax.broadcasted_iota(jnp.int32, (8, LANES), 0) < NVEC
    for v in range(slots // 2):
        a, b = 2 * v, 2 * v + 1
        here = pl.ds(8 * v, 8)
        rid_vm[here, :] = jnp.where(upper, index_sm[0, 0, 0, a], index_sm[0, 0, 0, b])
        cid_vm[here, :] = jnp.where(upper, index_sm[1, 0, 0, a], index_sm[1, 0, 0, b])
        wt_vm[here, :] = jnp.where(
            upper, table_sm[index_sm[2, 0, 0, a]], table_sm[index_sm[2, 0, 0, b]])
    rid = rid_vm[...]
    cid = cid_vm[...]
    sub = lax.broadcasted_iota(jnp.int32, (depth, LANES), 0)
    lane = lax.broadcasted_iota(jnp.int32, (depth, LANES), 1)
    half = lax.div(lane, TILE)
    cid_piece, cid_block = lax.div(cid, blocks), lax.rem(cid, blocks)
    global_row = me_row * (n_col * blocks) + rid
    global_col = (cid_piece * n_col + me_col) * blocks + cid_block
    weight = jnp.where(global_row == global_col, 0.5, 1.0) * wt_vm[...]
    weight = jnp.where(lax.div(sub, NVEC) < count_sm[0, 0], weight, 0.0)

    pair = 2 * NVEC
    first = lax.div(sub, depth // 2)
    second = lax.rem(lax.div(sub, NVEC), 2)

    def places(block):
        spot = lax.div(block, 2)
        line, part = lax.div(spot, 2), lax.rem(spot, 2)
        stay = jnp.where(part == second, line, -1)
        move = jnp.where(part != second, line, -1)
        return stay, move, lax.rem(block, 2)

    stay_row, move_row, odd_row = places(rid)
    stay_col, move_col, odd_col = places(cid)
    row_weight = jnp.where(half == odd_row, weight, 0.0)
    col_weight = jnp.where(half == odd_col, weight, 0.0)

    def pick(x_vm, which, odd, want):
        for t in range(slots):
            pick_vm[t * NVEC:(t + 1) * NVEC, :] = x_vm[spot_sm[which, t]].astype(jnp.float32)
        both = pick_vm[...]
        moved = jnp.where(odd == want, both, pltpu.roll(both, TILE, 1))
        return jnp.where(half == want, moved, 0.0)

    def finish(values, odd, have, weights):
        return jnp.where(odd == have, values, pltpu.roll(values, TILE, 1)) * weights

    def place(k, stay, move, values):
        def total(at, line):
            terms = [
                jnp.where(at[v * pair:(v + 1) * pair] == line, values[v * pair:(v + 1) * pair], 0.0)
                for v in range(slots // 2)]
            while len(terms) > 1:
                terms = [sum(terms[i + 1:i + 2], terms[i]) for i in range(0, len(terms), 2)]
            return terms[0]

        each = chunk // pair
        return jnp.concatenate([
            total(stay, line) + pltpu.roll(total(move, line), NVEC, 0)
            for line in range(k * each, (k + 1) * each)], axis=0)

    sets = slots // 16
    blank = jnp.zeros((2 * pair, LANES), jnp.bfloat16)

    def at(b0, m, b1, a1):
        return ((b0 * sets + m) * 2 + b1) * 2 + a1

    def left(rows, spots):
        def two(group):
            return jnp.concatenate(
                [rows[v * pair:(v + 1) * pair] for v in group], axis=0).astype(jnp.bfloat16)
        return jnp.concatenate([
            jnp.concatenate([two(spots[0]), blank], axis=1),
            jnp.concatenate([blank, two(spots[1])], axis=1)], axis=0)

    def tiles(m):
        return jnp.concatenate([
            w_vm[(m * 2 + b1) * 4:(m * 2 + b1) * 4 + 4].reshape(4 * TILE, LANES)
            for b1 in range(2)], axis=1)

    def collect(found, spots, result):
        for n, v in enumerate(spots[0] + spots[1]):
            found[v] = result[n * pair:(n + 1) * pair]

    def scatter(me, total, where, source, first, stay, move, values, other):
        for k in range(total):
            source[k] = place(k, stay, move, values)

            def send(k=k):
                slot = first + lax.rem(me - k + total, total) - 1
                pltpu.make_async_remote_copy(
                    src_ref=source.at[k], dst_ref=part_vm.at[slot], send_sem=send_sem,
                    recv_sem=p_sem, device_id=where(k), device_id_type=MESH).start()

            if k == 0 and other:
                send()
            else:
                pl.when(me != k)(send)

    def forward(other):
        arrived(far_vm, x_col_sem)
        distant = pick(far_vm, 1, odd_col, first)
        found = [None] * (slots // 2)
        for m in range(sets):
            spots = [[[at(b0, m, b1, a1) for b0 in range(2)] for b1 in range(2)]
                     for a1 in range(2)]
            result = lax.dot_general(
                jnp.concatenate([left(distant, spots[0]), left(distant, spots[1])], axis=0),
                tiles(m), (((1,), (1,)), ((), ())), preferred_element_type=jnp.float32)
            for a1 in range(2):
                collect(found, spots[a1], result[
                    a1 * 4 * pair:(a1 + 1) * 4 * pair, a1 * LANES:(a1 + 1) * LANES])
        values = finish(jnp.concatenate(found, axis=0), odd_row, second, row_weight)
        scatter(me_col, n_col, along_col, row_send, 0, stay_row, move_row, values, other)

    def mirrored():
        arrived(near_vm.at[pl.ds(0, (n_col - 1) * groups)], x_row_sem)
        near = pick(near_vm, 0, odd_row, second)
        found = [None] * (slots // 2)
        for m in range(sets):
            spots = [[[at(b0, m, b1, a1) for b0 in range(2)] for a1 in range(2)]
                     for b1 in range(2)]
            result = jnp.dot(
                jnp.concatenate([left(near, spots[0]), left(near, spots[1])], axis=0),
                tiles(m), preferred_element_type=jnp.float32)
            for b1 in range(2):
                collect(found, spots[b1], result[
                    b1 * 4 * pair:(b1 + 1) * 4 * pair, b1 * LANES:(b1 + 1) * LANES])
        values = finish(jnp.concatenate(found, axis=0), odd_col, first, col_weight)
        scatter(
            me_row, n_row, along_row, col_send, n_col - 1, stay_col, move_col, values, False)

    arrived(part_vm.at[pl.ds(0, peers // 2)], send_sem)

    @pl.when(me_col == 0)
    def _():
        mirrored()
        forward(False)

    @pl.when(me_col > 0)
    def _():
        forward(True)
        mirrored()

    total = row_send[me_col] + col_send[me_row]
    arrived(part_vm, p_sem)
    for d in range(peers):
        total = total + part_vm[d]
    out_ref[...] = total
    arrived(part_vm, send_sem)


def per_device(vectors, tile_values, tile_rows, tile_cols, tile_scale, tile_count, scale_table):
    n_row = lax.axis_size("row")
    n_col = lax.axis_size("col")
    piece_len = vectors.shape[1]
    slots = tile_rows.shape[-1]
    groups = piece_len // LANES
    chunk = groups * NVEC
    depth = slots * NVEC
    x = vectors.reshape(NVEC, groups, LANES).transpose(1, 0, 2)
    w = tile_values.reshape(slots, TILE * TILE)
    dma = pltpu.SemaphoreType.DMA
    hbm = pl.BlockSpec(memory_space=pltpu.HBM)
    out = pl.pallas_call(
        functools.partial(kernel, n_row, n_col, slots, piece_len),
        out_shape=pltpu.VMEM((chunk, LANES), jnp.float32),
        in_specs=[hbm] * 5 + [pl.BlockSpec(memory_space=pltpu.SMEM), hbm],
        out_specs=pl.BlockSpec(memory_space=pltpu.VMEM),
        scratch_shapes=[
            pltpu.VMEM((n_col * groups, NVEC, LANES), jnp.bfloat16),
            pltpu.VMEM((n_row * groups, NVEC, LANES), jnp.bfloat16),
            pltpu.VMEM((slots, TILE * TILE), jnp.bfloat16),
            pltpu.VMEM((slots // 2, TILE, LANES), jnp.bfloat16),
            pltpu.SMEM((3,) + tile_rows.shape, jnp.int32),
            pltpu.SMEM(scale_table.shape, jnp.float32),
            pltpu.SMEM((2, slots), jnp.int32),
            pltpu.VMEM((depth, LANES), jnp.int32),
            pltpu.VMEM((depth, LANES), jnp.int32),
            pltpu.VMEM((depth, LANES), jnp.float32),
            pltpu.VMEM((depth, LANES), jnp.float32),
            pltpu.VMEM((n_col, chunk, LANES), jnp.float32),
            pltpu.VMEM((n_row, chunk, LANES), jnp.float32),
            pltpu.VMEM((n_col + n_row - 2, chunk, LANES), jnp.float32),
            pltpu.SemaphoreType.REGULAR, dma, dma, dma, dma, dma, dma,
        ],
        compiler_params=pltpu.CompilerParams(collective_id=0, has_side_effects=True),
        name="lanczos",
    )(x, w, tile_rows, tile_cols, tile_scale, tile_count, scale_table)
    return out.reshape(groups, NVEC, LANES).transpose(1, 0, 2).reshape(NVEC, piece_len)


def solution(mesh):
    return jax.shard_map(
        per_device,
        mesh=mesh,
        in_specs=(
            P(None, ("row", "col")),
            P("row", "col", None, None),
            P("row", "col", None),
            P("row", "col", None),
            P("row", "col", None),
            P("row", "col"),
            P(),
        ),
        out_specs=P(None, ("row", "col")),
        check_vma=False,
    )
```

```python
import functools

import jax
import jax.numpy as jnp
from jax import lax
from jax.experimental import pallas as pl
from jax.experimental.pallas import tpu as pltpu
from jax.sharding import PartitionSpec as P

TILE = 64
NVEC = 4
LANES = 128
MESH = pl.DeviceIdType.MESH


def relayout(slots, tv_vm, w_vm):
    across = slots // 2
    pack = LANES // TILE
    step = max(1, 2 * LANES // (pack * across))
    depth = pack * step * across
    r = lax.broadcasted_iota(jnp.int32, (depth, depth), 0)
    c = lax.broadcasted_iota(jnp.int32, (depth, depth), 1)
    slot, i = lax.div(r, pack * step), lax.rem(r, pack * step)
    source = (lax.rem(i, pack) * step + lax.div(i, pack)) * across + slot
    order = jnp.where(c == source, 1.0, 0.0).astype(jnp.bfloat16)
    low_half = lax.broadcasted_iota(jnp.int32, (across, LANES), 1) < TILE
    total = TILE * TILE // LANES
    for first in range(0, total, step):
        even, odd = [], []
        for g in range(first, first + step):
            part = tv_vm[:, g * LANES:(g + 1) * LANES].astype(jnp.float32)
            turned = pltpu.roll(part, TILE, 1)
            even.append(jnp.where(low_half, part[:across], turned[across:]).astype(jnp.bfloat16))
            odd.append(jnp.where(low_half, turned[:across], part[across:]).astype(jnp.bfloat16))
        moved = jnp.dot(
            order, jnp.concatenate(even + odd, axis=0), preferred_element_type=jnp.float32)
        w_vm[:, first * pack:(first + step) * pack, :] = moved.reshape(
            across, pack * step, LANES).astype(jnp.bfloat16)


def kernel(
    n_row, n_col, slots, piece_len,
    x_hbm, w_hbm, rows_hbm, cols_hbm, scale_hbm, count_sm, table_hbm,
    out_ref,
    near_vm, far_vm, tv_vm, w_vm, index_sm, table_sm, spot_sm,
    rid_vm, cid_vm, wt_vm, pick_vm, lead_vm, row_send, col_send, part_vm,
    ready_sem, own_sem, index_sem, send_sem, x_row_sem, x_col_sem, p_sem,
):
    me_row = lax.axis_index("row")
    me_col = lax.axis_index("col")
    blocks = piece_len // TILE
    chunk = piece_len * NVEC // LANES
    depth = slots * NVEC
    peers = n_row + n_col - 2
    groups = piece_len // LANES

    def piece(ref, slot):
        return ref.at[pl.ds(slot * groups, groups)]

    def arrived(ref, sem):
        pltpu.make_async_copy(ref, ref, sem).wait()

    def along_col(p):
        return (me_row, p)

    def along_row(p):
        return (p, me_col)

    quarter = n_row // 4

    def between(place, n):
        return jnp.where(lax.div(place, quarter) == n, 1, 0)

    def each(low, greet, act):
        cols = [(p, me_col, n_col, along_col) for p in range(n_col)]
        rows = [(p, me_row, n_row, along_row) for p in range(n_row)]
        if not low:
            cols, rows = cols[::-1], rows[::-1]
        for p, me, total, where in cols[:1] + rows[:1] + cols[1:2] + rows[1:] + cols[2:]:
            if (low and p == total - 1) or (not low and p == 0):
                continue
            meets = p < me if low else p > me
            level = p // quarter
            if where is along_row and level in (1, 2):
                unlike = lax.div(me, quarter) != 3 - level
                apart = jnp.logical_and(meets, unlike)
                late = jnp.logical_or(meets, lax.div(me, quarter) == 3 - level)
                meets = apart if low or greet else late
            pl.when(meets)(functools.partial(act, p, where, where is along_col))

    barrier = pltpu.get_barrier_semaphore()

    def enter(p, place, is_col):
        pl.semaphore_signal(barrier, inc=1, device_id=place(p), device_id_type=MESH)

    def answer(p, place, is_col):
        pl.semaphore_signal(ready_sem, inc=1, device_id=place(p), device_id_type=MESH)

    def spread(p, place, is_col):
        pltpu.make_async_remote_copy(
            src_ref=piece(near_vm, me_col),
            dst_ref=piece(near_vm, me_col) if is_col else piece(far_vm, me_row), send_sem=send_sem,
            recv_sem=x_row_sem if is_col else x_col_sem,
            device_id=place(p), device_id_type=MESH).start()

    own = pltpu.make_async_copy(x_hbm, piece(near_vm, me_col), own_sem)
    again = pltpu.make_async_copy(x_hbm, piece(far_vm, me_row), x_col_sem)
    tiles_in = pltpu.make_async_copy(w_hbm, tv_vm, own_sem)
    table_in = pltpu.make_async_copy(table_hbm, table_sm, index_sem)
    own.start()
    each(False, True, enter)
    again.start()
    for i, src in enumerate((rows_hbm, cols_hbm, scale_hbm)):
        pltpu.make_async_copy(src, index_sm.at[i], index_sem).start()
    lower = me_row + me_col - quarter * between(me_row, 2)
    higher = peers - me_row - me_col - quarter * between(me_row, 1)

    @pl.when(lower > 0)
    def _():
        pl.semaphore_wait(barrier, lower)

    each(True, True, answer)
    own.wait()
    each(True, False, spread)
    tiles_in.start()
    arrived(index_sm, index_sem)
    table_in.start()

    @pl.when(higher > 0)
    def _():
        pl.semaphore_wait(ready_sem, higher)

    each(False, False, spread)

    tiles_in.wait()
    relayout(slots, tv_vm, w_vm)
    table_in.wait()
    for t in range(slots):
        spot_sm[0, t] = lax.shift_right_logical(index_sm[0, 0, 0, t], 1)
        spot_sm[1, t] = lax.shift_right_logical(index_sm[1, 0, 0, t], 1)
    upper = lax.broadcasted_iota(jnp.int32, (8, LANES), 0) < NVEC
    for v in range(slots // 2):
        a, b = 2 * v, 2 * v + 1
        here = pl.ds(8 * v, 8)
        rid_vm[here, :] = jnp.where(upper, index_sm[0, 0, 0, a], index_sm[0, 0, 0, b])
        cid_vm[here, :] = jnp.where(upper, index_sm[1, 0, 0, a], index_sm[1, 0, 0, b])
        wt_vm[here, :] = jnp.where(
            upper, table_sm[index_sm[2, 0, 0, a]], table_sm[index_sm[2, 0, 0, b]])
    rid = rid_vm[...]
    cid = cid_vm[...]
    sub = lax.broadcasted_iota(jnp.int32, (depth, LANES), 0)
    lane = lax.broadcasted_iota(jnp.int32, (depth, LANES), 1)
    half = lax.div(lane, TILE)
    cid_piece, cid_block = lax.div(cid, blocks), lax.rem(cid, blocks)
    global_row = me_row * (n_col * blocks) + rid
    global_col = (cid_piece * n_col + me_col) * blocks + cid_block
    weight = jnp.where(global_row == global_col, 0.5, 1.0) * wt_vm[...]
    weight = jnp.where(lax.div(sub, NVEC) < count_sm[0, 0], weight, 0.0)

    pair = 2 * NVEC
    first = lax.div(sub, depth // 2)
    second = lax.rem(lax.div(sub, NVEC), 2)

    def places(block):
        spot = lax.div(block, 2)
        line, part = lax.div(spot, 2), lax.rem(spot, 2)
        stay = jnp.where(part == second, line, -1)
        move = jnp.where(part != second, line, -1)
        return stay, move, lax.rem(block, 2)

    stay_row, move_row, odd_row = places(rid)
    stay_col, move_col, odd_col = places(cid)
    row_weight = jnp.where(half == odd_row, weight, 0.0)
    col_weight = jnp.where(half == odd_col, weight, 0.0)

    def pick(x_vm, which, odd, want):
        for t in range(slots):
            pick_vm[t * NVEC:(t + 1) * NVEC, :] = x_vm[spot_sm[which, t]].astype(jnp.float32)
        both = pick_vm[...]
        moved = jnp.where(odd == want, both, pltpu.roll(both, TILE, 1))
        return jnp.where(half == want, moved, 0.0)

    each = chunk // pair
    for way, stay, move, weights in (
            (0, stay_row, move_row, row_weight), (1, stay_col, move_col, col_weight)):
        for line in range(each):
            lead_vm[way, 2 * line] = jnp.where(stay == line, weights, 0.0)
            lead_vm[way, 2 * line + 1] = jnp.where(move == line, weights, 0.0)

    def finish(values, odd, have):
        return jnp.where(odd == have, values, pltpu.roll(values, TILE, 1))

    def tree(terms):
        while len(terms) > 1:
            terms = [sum(terms[i + 1:i + 2], terms[i]) for i in range(0, len(terms), 2)]
        return terms[0]

    def blocks_of(values):
        return [values[v * pair:(v + 1) * pair] for v in range(slots // 2)]

    def place_first(way, values):
        def total(n):
            return tree([a * b for a, b in zip(blocks_of(values), blocks_of(lead_vm[way, n]))])

        return jnp.concatenate([
            total(2 * line) + pltpu.roll(total(2 * line + 1), NVEC, 0)
            for line in range(each)], axis=0)

    def place(k, stay, move, values):
        def total(at, line):
            return tree([
                jnp.where(a == line, b, 0.0) for a, b in zip(blocks_of(at), blocks_of(values))])

        return jnp.concatenate([
            total(stay, line) + pltpu.roll(total(move, line), NVEC, 0)
            for line in range(k * each, (k + 1) * each)], axis=0)

    sets = slots // 16
    blank = jnp.zeros((2 * pair, LANES), jnp.bfloat16)

    def at(b0, m, b1, a1):
        return ((b0 * sets + m) * 2 + b1) * 2 + a1

    def left(rows, spots):
        def two(group):
            return jnp.concatenate(
                [rows[v * pair:(v + 1) * pair] for v in group], axis=0).astype(jnp.bfloat16)
        return jnp.concatenate([
            jnp.concatenate([two(spots[0]), blank], axis=1),
            jnp.concatenate([blank, two(spots[1])], axis=1)], axis=0)

    def tiles(m):
        return jnp.concatenate([
            w_vm[(m * 2 + b1) * 4:(m * 2 + b1) * 4 + 4].reshape(4 * TILE, LANES)
            for b1 in range(2)], axis=1)

    def collect(found, spots, result):
        for n, v in enumerate(spots[0] + spots[1]):
            found[v] = result[n * pair:(n + 1) * pair]

    def scatter(me, total, where, source, first, way, stay, move, weights, values, other):
        def part(k, placed, sure=False):
            source[k] = placed

            def send():
                slot = first + lax.rem(me - k + total, total) - 1
                pltpu.make_async_remote_copy(
                    src_ref=source.at[k], dst_ref=part_vm.at[slot], send_sem=send_sem,
                    recv_sem=p_sem, device_id=where(k), device_id_type=MESH).start()

            if sure:
                send()
            else:
                pl.when(me != k)(send)

        part(0, place_first(way, values), other)

        @pl.when(me >= 0)
        def _():
            weighted = values * weights
            for k in range(1, total):
                part(k, place(k, stay, move, weighted))

    def forward(other):
        arrived(far_vm, x_col_sem)
        distant = pick(far_vm, 1, odd_col, first)
        found = [None] * (slots // 2)
        for m in range(sets):
            spots = [[[at(b0, m, b1, a1) for b0 in range(2)] for b1 in range(2)]
                     for a1 in range(2)]
            result = lax.dot_general(
                jnp.concatenate([left(distant, spots[0]), left(distant, spots[1])], axis=0),
                tiles(m), (((1,), (1,)), ((), ())), preferred_element_type=jnp.float32)
            for a1 in range(2):
                collect(found, spots[a1], result[
                    a1 * 4 * pair:(a1 + 1) * 4 * pair, a1 * LANES:(a1 + 1) * LANES])
        values = finish(jnp.concatenate(found, axis=0), odd_row, second)
        scatter(me_col, n_col, along_col, row_send, 0, 0, stay_row, move_row, row_weight, values,
            other)

    def mirrored():
        arrived(near_vm.at[pl.ds(0, (n_col - 1) * groups)], x_row_sem)
        near = pick(near_vm, 0, odd_row, second)
        found = [None] * (slots // 2)
        for m in range(sets):
            spots = [[[at(b0, m, b1, a1) for b0 in range(2)] for a1 in range(2)]
                     for b1 in range(2)]
            result = jnp.dot(
                jnp.concatenate([left(near, spots[0]), left(near, spots[1])], axis=0),
                tiles(m), preferred_element_type=jnp.float32)
            for b1 in range(2):
                collect(found, spots[b1], result[
                    b1 * 4 * pair:(b1 + 1) * 4 * pair, b1 * LANES:(b1 + 1) * LANES])
        values = finish(jnp.concatenate(found, axis=0), odd_col, first)
        scatter(
            me_row, n_row, along_row, col_send, n_col - 1, 1, stay_col, move_col, col_weight, values,
            False)

    arrived(part_vm.at[pl.ds(0, peers // 2)], send_sem)

    @pl.when(me_col == 0)
    def _():
        mirrored()
        forward(False)

    @pl.when(me_col > 0)
    def _():
        forward(True)
        mirrored()

    total = row_send[me_col] + col_send[me_row]
    arrived(part_vm, p_sem)
    for d in range(peers):
        total = total + part_vm[d]
    out_ref[...] = total
    arrived(part_vm, send_sem)


def per_device(vectors, tile_values, tile_rows, tile_cols, tile_scale, tile_count, scale_table):
    n_row = lax.axis_size("row")
    n_col = lax.axis_size("col")
    piece_len = vectors.shape[1]
    slots = tile_rows.shape[-1]
    groups = piece_len // LANES
    chunk = groups * NVEC
    depth = slots * NVEC
    x = vectors.reshape(NVEC, groups, LANES).transpose(1, 0, 2)
    w = tile_values.reshape(slots, TILE * TILE)
    dma = pltpu.SemaphoreType.DMA
    hbm = pl.BlockSpec(memory_space=pltpu.HBM)
    out = pl.pallas_call(
        functools.partial(kernel, n_row, n_col, slots, piece_len),
        out_shape=pltpu.VMEM((chunk, LANES), jnp.float32),
        in_specs=[hbm] * 5 + [pl.BlockSpec(memory_space=pltpu.SMEM), hbm],
        out_specs=pl.BlockSpec(memory_space=pltpu.VMEM),
        scratch_shapes=[
            pltpu.VMEM((n_col * groups, NVEC, LANES), jnp.bfloat16),
            pltpu.VMEM((n_row * groups, NVEC, LANES), jnp.bfloat16),
            pltpu.VMEM((slots, TILE * TILE), jnp.bfloat16),
            pltpu.VMEM((slots // 2, TILE, LANES), jnp.bfloat16),
            pltpu.SMEM((3,) + tile_rows.shape, jnp.int32),
            pltpu.SMEM(scale_table.shape, jnp.float32),
            pltpu.SMEM((2, slots), jnp.int32),
            pltpu.VMEM((depth, LANES), jnp.int32),
            pltpu.VMEM((depth, LANES), jnp.int32),
            pltpu.VMEM((depth, LANES), jnp.float32),
            pltpu.VMEM((depth, LANES), jnp.float32),
            pltpu.VMEM((2, 2 * chunk // (2 * NVEC), depth, LANES), jnp.float32),
            pltpu.VMEM((n_col, chunk, LANES), jnp.float32),
            pltpu.VMEM((n_row, chunk, LANES), jnp.float32),
            pltpu.VMEM((n_col + n_row - 2, chunk, LANES), jnp.float32),
            pltpu.SemaphoreType.REGULAR, dma, dma, dma, dma, dma, dma,
        ],
        compiler_params=pltpu.CompilerParams(collective_id=0, has_side_effects=True),
        name="lanczos",
    )(x, w, tile_rows, tile_cols, tile_scale, tile_count, scale_table)
    return out.reshape(groups, NVEC, LANES).transpose(1, 0, 2).reshape(NVEC, piece_len)


def solution(mesh):
    return jax.shard_map(
        per_device,
        mesh=mesh,
        in_specs=(
            P(None, ("row", "col")),
            P("row", "col", None, None),
            P("row", "col", None),
            P("row", "col", None),
            P("row", "col", None),
            P("row", "col"),
            P(),
        ),
        out_specs=P(None, ("row", "col")),
        check_vma=False,
    )
```

```python
import functools

import jax
import jax.numpy as jnp
from jax import lax
from jax.experimental import pallas as pl
from jax.experimental.pallas import tpu as pltpu
from jax.sharding import PartitionSpec as P

TILE = 64
NVEC = 4
LANES = 128
MESH = pl.DeviceIdType.MESH


def relayout(slots, tv_vm, w_vm):
    across = slots // 2
    pack = LANES // TILE
    step = max(1, 2 * LANES // (pack * across))
    depth = pack * step * across
    r = lax.broadcasted_iota(jnp.int32, (depth, depth), 0)
    c = lax.broadcasted_iota(jnp.int32, (depth, depth), 1)
    slot, i = lax.div(r, pack * step), lax.rem(r, pack * step)
    source = (lax.rem(i, pack) * step + lax.div(i, pack)) * across + slot
    order = jnp.where(c == source, 1.0, 0.0).astype(jnp.bfloat16)
    low_half = lax.broadcasted_iota(jnp.int32, (across, LANES), 1) < TILE
    total = TILE * TILE // LANES
    for first in range(0, total, step):
        even, odd = [], []
        for g in range(first, first + step):
            part = tv_vm[:, g * LANES:(g + 1) * LANES].astype(jnp.float32)
            turned = pltpu.roll(part, TILE, 1)
            even.append(jnp.where(low_half, part[:across], turned[across:]).astype(jnp.bfloat16))
            odd.append(jnp.where(low_half, turned[:across], part[across:]).astype(jnp.bfloat16))
        moved = jnp.dot(
            order, jnp.concatenate(even + odd, axis=0), preferred_element_type=jnp.float32)
        w_vm[:, first * pack:(first + step) * pack, :] = moved.reshape(
            across, pack * step, LANES).astype(jnp.bfloat16)


def kernel(
    n_row, n_col, slots, piece_len,
    x_hbm, w_hbm, rows_hbm, cols_hbm, scale_hbm, count_sm, table_hbm,
    out_ref,
    near_vm, far_vm, tv_vm, w_vm, index_sm, table_sm, spot_sm,
    rid_vm, cid_vm, wt_vm, pick_vm, lead_vm, row_send, col_send, part_vm,
    ready_sem, own_sem, index_sem, send_sem, x_row_sem, x_col_sem, p_sem,
):
    me_row = lax.axis_index("row")
    me_col = lax.axis_index("col")
    blocks = piece_len // TILE
    chunk = piece_len * NVEC // LANES
    depth = slots * NVEC
    peers = n_row + n_col - 2
    groups = piece_len // LANES

    def piece(ref, slot):
        return ref.at[pl.ds(slot * groups, groups)]

    def arrived(ref, sem):
        pltpu.make_async_copy(ref, ref, sem).wait()

    def along_col(p):
        return (me_row, p)

    def along_row(p):
        return (p, me_col)

    quarter = n_row // 4

    def between(place, n):
        return jnp.where(lax.div(place, quarter) == n, 1, 0)

    def each(low, greet, act):
        cols = [(p, me_col, n_col, along_col) for p in range(n_col)]
        rows = [(p, me_row, n_row, along_row) for p in range(n_row)]
        if not low:
            cols, rows = cols[::-1], rows[::-1]
        for p, me, total, where in cols[:1] + rows[:1] + cols[1:2] + rows[1:] + cols[2:]:
            if (low and p == total - 1) or (not low and p == 0):
                continue
            meets = p < me if low else p > me
            level = p // quarter
            if where is along_row and level in (1, 2):
                unlike = lax.div(me, quarter) != 3 - level
                apart = jnp.logical_and(meets, unlike)
                late = jnp.logical_or(meets, lax.div(me, quarter) == 3 - level)
                meets = apart if low or greet else late
            pl.when(meets)(functools.partial(act, p, where, where is along_col))

    barrier = pltpu.get_barrier_semaphore()

    def enter(p, place, is_col):
        pl.semaphore_signal(barrier, inc=1, device_id=place(p), device_id_type=MESH)

    def answer(p, place, is_col):
        pl.semaphore_signal(ready_sem, inc=1, device_id=place(p), device_id_type=MESH)

    def spread(p, place, is_col):
        pltpu.make_async_remote_copy(
            src_ref=piece(near_vm, me_col),
            dst_ref=piece(near_vm, me_col) if is_col else piece(far_vm, me_row), send_sem=send_sem,
            recv_sem=x_row_sem if is_col else x_col_sem,
            device_id=place(p), device_id_type=MESH).start()

    own = pltpu.make_async_copy(x_hbm, piece(near_vm, me_col), own_sem)
    again = pltpu.make_async_copy(x_hbm, piece(far_vm, me_row), x_col_sem)
    tiles_in = pltpu.make_async_copy(w_hbm, tv_vm, own_sem)
    table_in = pltpu.make_async_copy(table_hbm, table_sm, index_sem)
    own.start()
    each(False, True, enter)
    again.start()
    for i, src in enumerate((rows_hbm, cols_hbm, scale_hbm)):
        pltpu.make_async_copy(src, index_sm.at[i], index_sem).start()
    lower = me_row + me_col - quarter * between(me_row, 2)
    higher = peers - me_row - me_col - quarter * between(me_row, 1)

    @pl.when(lower > 0)
    def _():
        pl.semaphore_wait(barrier, lower)

    own.wait()
    each(True, False, spread)
    each(True, True, answer)
    tiles_in.start()
    arrived(index_sm, index_sem)
    table_in.start()

    @pl.when(higher > 0)
    def _():
        pl.semaphore_wait(ready_sem, higher)

    each(False, False, spread)

    tiles_in.wait()
    relayout(slots, tv_vm, w_vm)
    table_in.wait()
    for t in range(slots):
        spot_sm[0, t] = lax.shift_right_logical(index_sm[0, 0, 0, t], 1)
        spot_sm[1, t] = lax.shift_right_logical(index_sm[1, 0, 0, t], 1)
    upper = lax.broadcasted_iota(jnp.int32, (8, LANES), 0) < NVEC
    for v in range(slots // 2):
        a, b = 2 * v, 2 * v + 1
        here = pl.ds(8 * v, 8)
        rid_vm[here, :] = jnp.where(upper, index_sm[0, 0, 0, a], index_sm[0, 0, 0, b])
        cid_vm[here, :] = jnp.where(upper, index_sm[1, 0, 0, a], index_sm[1, 0, 0, b])
        wt_vm[here, :] = jnp.where(
            upper, table_sm[index_sm[2, 0, 0, a]], table_sm[index_sm[2, 0, 0, b]])
    rid = rid_vm[...]
    cid = cid_vm[...]
    sub = lax.broadcasted_iota(jnp.int32, (depth, LANES), 0)
    lane = lax.broadcasted_iota(jnp.int32, (depth, LANES), 1)
    half = lax.div(lane, TILE)
    cid_piece, cid_block = lax.div(cid, blocks), lax.rem(cid, blocks)
    global_row = me_row * (n_col * blocks) + rid
    global_col = (cid_piece * n_col + me_col) * blocks + cid_block
    weight = jnp.where(global_row == global_col, 0.5, 1.0) * wt_vm[...]
    weight = jnp.where(lax.div(sub, NVEC) < count_sm[0, 0], weight, 0.0)

    pair = 2 * NVEC
    first = lax.div(sub, depth // 2)
    second = lax.rem(lax.div(sub, NVEC), 2)

    def places(block):
        spot = lax.div(block, 2)
        line, part = lax.div(spot, 2), lax.rem(spot, 2)
        stay = jnp.where(part == second, line, -1)
        move = jnp.where(part != second, line, -1)
        return stay, move, lax.rem(block, 2)

    stay_row, move_row, odd_row = places(rid)
    stay_col, move_col, odd_col = places(cid)
    row_weight = jnp.where(half == odd_row, weight, 0.0)
    col_weight = jnp.where(half == odd_col, weight, 0.0)

    def pick(x_vm, which, odd, want):
        for t in range(slots):
            pick_vm[t * NVEC:(t + 1) * NVEC, :] = x_vm[spot_sm[which, t]].astype(jnp.float32)
        both = pick_vm[...]
        moved = jnp.where(odd == want, both, pltpu.roll(both, TILE, 1))
        return jnp.where(half == want, moved, 0.0)

    each = chunk // pair
    for way, stay, move, weights in (
            (0, stay_row, move_row, row_weight), (1, stay_col, move_col, col_weight)):
        for line in range(each):
            lead_vm[way, 2 * line] = jnp.where(stay == line, weights, 0.0)
            lead_vm[way, 2 * line + 1] = jnp.where(move == line, weights, 0.0)

    def finish(values, odd, have):
        return jnp.where(odd == have, values, pltpu.roll(values, TILE, 1))

    def tree(terms):
        while len(terms) > 1:
            terms = [sum(terms[i + 1:i + 2], terms[i]) for i in range(0, len(terms), 2)]
        return terms[0]

    def blocks_of(values):
        return [values[v * pair:(v + 1) * pair] for v in range(slots // 2)]

    def place_first(way, values):
        def total(n):
            return tree([a * b for a, b in zip(blocks_of(values), blocks_of(lead_vm[way, n]))])

        return jnp.concatenate([
            total(2 * line) + pltpu.roll(total(2 * line + 1), NVEC, 0)
            for line in range(each)], axis=0)

    def place(k, stay, move, values):
        def total(at, line):
            return tree([
                jnp.where(a == line, b, 0.0) for a, b in zip(blocks_of(at), blocks_of(values))])

        return jnp.concatenate([
            total(stay, line) + pltpu.roll(total(move, line), NVEC, 0)
            for line in range(k * each, (k + 1) * each)], axis=0)

    sets = slots // 16
    blank = jnp.zeros((2 * pair, LANES), jnp.bfloat16)

    def at(b0, m, b1, a1):
        return ((b0 * sets + m) * 2 + b1) * 2 + a1

    def left(rows, spots):
        def two(group):
            return jnp.concatenate(
                [rows[v * pair:(v + 1) * pair] for v in group], axis=0).astype(jnp.bfloat16)
        return jnp.concatenate([
            jnp.concatenate([two(spots[0]), blank], axis=1),
            jnp.concatenate([blank, two(spots[1])], axis=1)], axis=0)

    def tiles(m):
        return jnp.concatenate([
            w_vm[(m * 2 + b1) * 4:(m * 2 + b1) * 4 + 4].reshape(4 * TILE, LANES)
            for b1 in range(2)], axis=1)

    def collect(found, spots, result):
        for n, v in enumerate(spots[0] + spots[1]):
            found[v] = result[n * pair:(n + 1) * pair]

    def scatter(me, total, where, source, first, way, stay, move, weights, values, other):
        def part(k, placed, sure=False):
            source[k] = placed

            def send():
                slot = first + lax.rem(me - k + total, total) - 1
                pltpu.make_async_remote_copy(
                    src_ref=source.at[k], dst_ref=part_vm.at[slot], send_sem=send_sem,
                    recv_sem=p_sem, device_id=where(k), device_id_type=MESH).start()

            if sure:
                send()
            else:
                pl.when(me != k)(send)

        part(0, place_first(way, values), other)

        @pl.when(me >= 0)
        def _():
            weighted = values * weights
            for k in range(1, total):
                part(k, place(k, stay, move, weighted))

    def forward(other):
        arrived(far_vm, x_col_sem)
        distant = pick(far_vm, 1, odd_col, first)
        found = [None] * (slots // 2)
        for m in range(sets):
            spots = [[[at(b0, m, b1, a1) for b0 in range(2)] for b1 in range(2)]
                     for a1 in range(2)]
            result = lax.dot_general(
                jnp.concatenate([left(distant, spots[0]), left(distant, spots[1])], axis=0),
                tiles(m), (((1,), (1,)), ((), ())), preferred_element_type=jnp.float32)
            for a1 in range(2):
                collect(found, spots[a1], result[
                    a1 * 4 * pair:(a1 + 1) * 4 * pair, a1 * LANES:(a1 + 1) * LANES])
        values = finish(jnp.concatenate(found, axis=0), odd_row, second)
        scatter(me_col, n_col, along_col, row_send, 0, 0, stay_row, move_row, row_weight, values,
            other)

    def mirrored():
        arrived(near_vm.at[pl.ds(0, (n_col - 1) * groups)], x_row_sem)
        near = pick(near_vm, 0, odd_row, second)
        found = [None] * (slots // 2)
        for m in range(sets):
            spots = [[[at(b0, m, b1, a1) for b0 in range(2)] for a1 in range(2)]
                     for b1 in range(2)]
            result = jnp.dot(
                jnp.concatenate([left(near, spots[0]), left(near, spots[1])], axis=0),
                tiles(m), preferred_element_type=jnp.float32)
            for b1 in range(2):
                collect(found, spots[b1], result[
                    b1 * 4 * pair:(b1 + 1) * 4 * pair, b1 * LANES:(b1 + 1) * LANES])
        values = finish(jnp.concatenate(found, axis=0), odd_col, first)
        scatter(
            me_row, n_row, along_row, col_send, n_col - 1, 1, stay_col, move_col, col_weight, values,
            False)

    arrived(part_vm.at[pl.ds(0, peers // 2)], send_sem)

    @pl.when(me_col == 0)
    def _():
        mirrored()
        forward(False)

    @pl.when(me_col > 0)
    def _():
        forward(True)
        mirrored()

    total = row_send[me_col] + col_send[me_row]
    arrived(part_vm, p_sem)
    for d in range(peers):
        total = total + part_vm[d]
    out_ref[...] = total
    arrived(part_vm, send_sem)


def per_device(vectors, tile_values, tile_rows, tile_cols, tile_scale, tile_count, scale_table):
    n_row = lax.axis_size("row")
    n_col = lax.axis_size("col")
    piece_len = vectors.shape[1]
    slots = tile_rows.shape[-1]
    groups = piece_len // LANES
    chunk = groups * NVEC
    depth = slots * NVEC
    x = vectors.reshape(NVEC, groups, LANES).transpose(1, 0, 2)
    w = tile_values.reshape(slots, TILE * TILE)
    dma = pltpu.SemaphoreType.DMA
    hbm = pl.BlockSpec(memory_space=pltpu.HBM)
    out = pl.pallas_call(
        functools.partial(kernel, n_row, n_col, slots, piece_len),
        out_shape=pltpu.VMEM((chunk, LANES), jnp.float32),
        in_specs=[hbm] * 5 + [pl.BlockSpec(memory_space=pltpu.SMEM), hbm],
        out_specs=pl.BlockSpec(memory_space=pltpu.VMEM),
        scratch_shapes=[
            pltpu.VMEM((n_col * groups, NVEC, LANES), jnp.bfloat16),
            pltpu.VMEM((n_row * groups, NVEC, LANES), jnp.bfloat16),
            pltpu.VMEM((slots, TILE * TILE), jnp.bfloat16),
            pltpu.VMEM((slots // 2, TILE, LANES), jnp.bfloat16),
            pltpu.SMEM((3,) + tile_rows.shape, jnp.int32),
            pltpu.SMEM(scale_table.shape, jnp.float32),
            pltpu.SMEM((2, slots), jnp.int32),
            pltpu.VMEM((depth, LANES), jnp.int32),
            pltpu.VMEM((depth, LANES), jnp.int32),
            pltpu.VMEM((depth, LANES), jnp.float32),
            pltpu.VMEM((depth, LANES), jnp.float32),
            pltpu.VMEM((2, 2 * chunk // (2 * NVEC), depth, LANES), jnp.float32),
            pltpu.VMEM((n_col, chunk, LANES), jnp.float32),
            pltpu.VMEM((n_row, chunk, LANES), jnp.float32),
            pltpu.VMEM((n_col + n_row - 2, chunk, LANES), jnp.float32),
            pltpu.SemaphoreType.REGULAR, dma, dma, dma, dma, dma, dma,
        ],
        compiler_params=pltpu.CompilerParams(collective_id=0, has_side_effects=True),
        name="lanczos",
    )(x, w, tile_rows, tile_cols, tile_scale, tile_count, scale_table)
    return out.reshape(groups, NVEC, LANES).transpose(1, 0, 2).reshape(NVEC, piece_len)


def solution(mesh):
    return jax.shard_map(
        per_device,
        mesh=mesh,
        in_specs=(
            P(None, ("row", "col")),
            P("row", "col", None, None),
            P("row", "col", None),
            P("row", "col", None),
            P("row", "col", None),
            P("row", "col"),
            P(),
        ),
        out_specs=P(None, ("row", "col")),
        check_vma=False,
    )
```

```python
import functools

import jax
import jax.numpy as jnp
from jax import lax
from jax.experimental import pallas as pl
from jax.experimental.pallas import tpu as pltpu
from jax.sharding import PartitionSpec as P

TILE = 64
NVEC = 4
LANES = 128
MESH = pl.DeviceIdType.MESH


def relayout(slots, tv_vm, w_vm):
    across = slots // 2
    pack = LANES // TILE
    step = max(1, 2 * LANES // (pack * across))
    depth = pack * step * across
    r = lax.broadcasted_iota(jnp.int32, (depth, depth), 0)
    c = lax.broadcasted_iota(jnp.int32, (depth, depth), 1)
    slot, i = lax.div(r, pack * step), lax.rem(r, pack * step)
    source = (lax.rem(i, pack) * step + lax.div(i, pack)) * across + slot
    order = jnp.where(c == source, 1.0, 0.0).astype(jnp.bfloat16)
    low_half = lax.broadcasted_iota(jnp.int32, (across, LANES), 1) < TILE
    total = TILE * TILE // LANES
    for first in range(0, total, step):
        even, odd = [], []
        for g in range(first, first + step):
            part = tv_vm[:, g * LANES:(g + 1) * LANES].astype(jnp.float32)
            turned = pltpu.roll(part, TILE, 1)
            even.append(jnp.where(low_half, part[:across], turned[across:]).astype(jnp.bfloat16))
            odd.append(jnp.where(low_half, turned[:across], part[across:]).astype(jnp.bfloat16))
        moved = jnp.dot(
            order, jnp.concatenate(even + odd, axis=0), preferred_element_type=jnp.float32)
        w_vm[:, first * pack:(first + step) * pack, :] = moved.reshape(
            across, pack * step, LANES).astype(jnp.bfloat16)


def kernel(
    n_row, n_col, slots, piece_len,
    x_hbm, w_hbm, rows_hbm, cols_hbm, scale_hbm, count_sm, table_hbm,
    out_ref,
    near_vm, far_vm, tv_vm, w_vm, index_sm, table_sm, spot_sm,
    rid_vm, cid_vm, wt_vm, pick_vm, lead_vm, row_send, col_send, part_vm,
    ready_sem, own_sem, index_sem, send_sem, x_row_sem, x_col_sem, p_sem,
):
    me_row = lax.axis_index("row")
    me_col = lax.axis_index("col")
    blocks = piece_len // TILE
    chunk = piece_len * NVEC // LANES
    depth = slots * NVEC
    peers = n_row + n_col - 2
    groups = piece_len // LANES

    def piece(ref, slot):
        return ref.at[pl.ds(slot * groups, groups)]

    def arrived(ref, sem):
        pltpu.make_async_copy(ref, ref, sem).wait()

    def along_col(p):
        return (me_row, p)

    def along_row(p):
        return (p, me_col)

    quarter = n_row // 4

    def between(place, n):
        return jnp.where(lax.div(place, quarter) == n, 1, 0)

    def each(low, greet, act):
        cols = [(p, me_col, n_col, along_col) for p in range(n_col)]
        rows = [(p, me_row, n_row, along_row) for p in range(n_row)]
        if not low:
            cols, rows = cols[::-1], rows[::-1]
        for p, me, total, where in cols[:1] + rows[:1] + cols[1:2] + rows[1:] + cols[2:]:
            if (low and p == total - 1) or (not low and p == 0):
                continue
            meets = p < me if low else p > me
            level = p // quarter
            if where is along_row and level in (1, 2):
                unlike = lax.div(me, quarter) != 3 - level
                apart = jnp.logical_and(meets, unlike)
                late = jnp.logical_or(meets, lax.div(me, quarter) == 3 - level)
                meets = apart if low or greet else late
            pl.when(meets)(functools.partial(act, p, where, where is along_col))

    barrier = pltpu.get_barrier_semaphore()

    def enter(p, place, is_col):
        pl.semaphore_signal(barrier, inc=1, device_id=place(p), device_id_type=MESH)

    def answer(p, place, is_col):
        pl.semaphore_signal(ready_sem, inc=1, device_id=place(p), device_id_type=MESH)

    def spread(p, place, is_col):
        pltpu.make_async_remote_copy(
            src_ref=piece(near_vm, me_col),
            dst_ref=piece(near_vm, me_col) if is_col else piece(far_vm, me_row), send_sem=send_sem,
            recv_sem=x_row_sem if is_col else x_col_sem,
            device_id=place(p), device_id_type=MESH).start()

    own = pltpu.make_async_copy(x_hbm, piece(near_vm, me_col), own_sem)
    again = pltpu.make_async_copy(x_hbm, piece(far_vm, me_row), x_col_sem)
    tiles_in = pltpu.make_async_copy(w_hbm, tv_vm, own_sem)
    table_in = pltpu.make_async_copy(table_hbm, table_sm, index_sem)
    own.start()
    each(False, True, enter)
    again.start()
    for i, src in enumerate((rows_hbm, cols_hbm, scale_hbm)):
        pltpu.make_async_copy(src, index_sm.at[i], index_sem).start()
    lower = me_row + me_col - quarter * between(me_row, 2)
    higher = peers - me_row - me_col - quarter * between(me_row, 1)

    @pl.when(lower > 0)
    def _():
        pl.semaphore_wait(barrier, lower)

    own.wait()
    each(True, False, spread)
    each(True, True, answer)
    tiles_in.start()
    arrived(index_sm, index_sem)
    table_in.start()

    @pl.when(higher > 0)
    def _():
        pl.semaphore_wait(ready_sem, higher)

    each(False, False, spread)

    tiles_in.wait()
    relayout(slots, tv_vm, w_vm)
    table_in.wait()
    for t in range(slots):
        spot_sm[0, t] = lax.shift_right_logical(index_sm[0, 0, 0, t], 1)
        spot_sm[1, t] = lax.shift_right_logical(index_sm[1, 0, 0, t], 1)
    upper = lax.broadcasted_iota(jnp.int32, (8, LANES), 0) < NVEC
    for v in range(slots // 2):
        a, b = 2 * v, 2 * v + 1
        here = pl.ds(8 * v, 8)
        rid_vm[here, :] = jnp.where(upper, index_sm[0, 0, 0, a], index_sm[0, 0, 0, b])
        cid_vm[here, :] = jnp.where(upper, index_sm[1, 0, 0, a], index_sm[1, 0, 0, b])
        wt_vm[here, :] = jnp.where(
            upper, table_sm[index_sm[2, 0, 0, a]], table_sm[index_sm[2, 0, 0, b]])
    rid = rid_vm[...]
    cid = cid_vm[...]
    sub = lax.broadcasted_iota(jnp.int32, (depth, LANES), 0)
    lane = lax.broadcasted_iota(jnp.int32, (depth, LANES), 1)
    half = lax.div(lane, TILE)
    cid_piece, cid_block = lax.div(cid, blocks), lax.rem(cid, blocks)
    global_row = me_row * (n_col * blocks) + rid
    global_col = (cid_piece * n_col + me_col) * blocks + cid_block
    weight = jnp.where(global_row == global_col, 0.5, 1.0) * wt_vm[...]
    weight = jnp.where(lax.div(sub, NVEC) < count_sm[0, 0], weight, 0.0)

    pair = 2 * NVEC
    first = lax.div(sub, depth // 2)
    second = lax.rem(lax.div(sub, NVEC), 2)

    def places(block):
        spot = lax.div(block, 2)
        line, part = lax.div(spot, 2), lax.rem(spot, 2)
        stay = jnp.where(part == second, line, -1)
        move = jnp.where(part != second, line, -1)
        return stay, move, lax.rem(block, 2)

    stay_row, move_row, odd_row = places(rid)
    stay_col, move_col, odd_col = places(cid)
    row_weight = jnp.where(half == odd_row, weight, 0.0)
    col_weight = jnp.where(half == odd_col, weight, 0.0)

    def pick(x_vm, which, odd, want):
        for t in range(slots):
            pick_vm[t * NVEC:(t + 1) * NVEC, :] = x_vm[spot_sm[which, t]].astype(jnp.float32)
        both = pick_vm[...]
        moved = jnp.where(odd == want, both, pltpu.roll(both, TILE, 1))
        return jnp.where(half == want, moved, 0.0)

    each = chunk // pair
    for way, stay, move, weights in (
            (0, stay_row, move_row, row_weight), (1, stay_col, move_col, col_weight)):
        for line in range(each):
            lead_vm[way, 2 * line] = jnp.where(stay == line, weights, 0.0)
            lead_vm[way, 2 * line + 1] = jnp.where(move == line, weights, 0.0)

    def finish(values, odd, have):
        return jnp.where(odd == have, values, pltpu.roll(values, TILE, 1))

    def tree(terms):
        while len(terms) > 1:
            terms = [sum(terms[i + 1:i + 2], terms[i]) for i in range(0, len(terms), 2)]
        return terms[0]

    def blocks_of(values):
        return [values[v * pair:(v + 1) * pair] for v in range(slots // 2)]

    def place_first(way, values):
        def total(n):
            return tree([a * b for a, b in zip(blocks_of(values), blocks_of(lead_vm[way, n]))])

        return jnp.concatenate([
            total(2 * line) + pltpu.roll(total(2 * line + 1), NVEC, 0)
            for line in range(each)], axis=0)

    def place(k, stay, move, values):
        def total(at, line):
            return tree([
                jnp.where(a == line, b, 0.0) for a, b in zip(blocks_of(at), blocks_of(values))])

        return jnp.concatenate([
            total(stay, line) + pltpu.roll(total(move, line), NVEC, 0)
            for line in range(k * each, (k + 1) * each)], axis=0)

    sets = slots // 16
    blank = jnp.zeros((2 * pair, LANES), jnp.bfloat16)

    def at(b0, m, b1, a1):
        return ((b0 * sets + m) * 2 + b1) * 2 + a1

    def left(rows, spots):
        def two(group):
            return jnp.concatenate(
                [rows[v * pair:(v + 1) * pair] for v in group], axis=0).astype(jnp.bfloat16)
        return jnp.concatenate([
            jnp.concatenate([two(spots[0]), blank], axis=1),
            jnp.concatenate([blank, two(spots[1])], axis=1)], axis=0)

    def tiles(m):
        return jnp.concatenate([
            w_vm[(m * 2 + b1) * 4:(m * 2 + b1) * 4 + 4].reshape(4 * TILE, LANES)
            for b1 in range(2)], axis=1)

    def collect(found, spots, result):
        for n, v in enumerate(spots[0] + spots[1]):
            found[v] = result[n * pair:(n + 1) * pair]

    def scatter(me, total, where, source, first, way, stay, move, weights, values, other):
        def part(k, placed, sure=False):
            source[k] = placed

            def send():
                slot = first + lax.rem(me - k + total, total) - 1
                pltpu.make_async_remote_copy(
                    src_ref=source.at[k], dst_ref=part_vm.at[slot], send_sem=send_sem,
                    recv_sem=p_sem, device_id=where(k), device_id_type=MESH).start()

            if sure:
                send()
            else:
                pl.when(me != k)(send)

        part(0, place_first(way, values), other)

        @pl.when(me >= 0)
        def _():
            weighted = values * weights
            for k in range(1, total):
                part(k, place(k, stay, move, weighted))

    def forward(other):
        arrived(far_vm, x_col_sem)
        distant = pick(far_vm, 1, odd_col, first)
        found = [None] * (slots // 2)
        for m in range(sets):
            spots = [[[at(b0, m, b1, a1) for b0 in range(2)] for b1 in range(2)]
                     for a1 in range(2)]
            result = lax.dot_general(
                jnp.concatenate([left(distant, spots[0]), left(distant, spots[1])], axis=0),
                tiles(m), (((1,), (1,)), ((), ())), preferred_element_type=jnp.float32)
            for a1 in range(2):
                collect(found, spots[a1], result[
                    a1 * 4 * pair:(a1 + 1) * 4 * pair, a1 * LANES:(a1 + 1) * LANES])
        values = finish(jnp.concatenate(found, axis=0), odd_row, second)
        scatter(me_col, n_col, along_col, row_send, 0, 0, stay_row, move_row, row_weight, values,
            other)

    def mirrored():
        arrived(near_vm.at[pl.ds(0, (n_col - 1) * groups)], x_row_sem)
        near = pick(near_vm, 0, odd_row, second)
        found = [None] * (slots // 2)
        for m in range(sets):
            spots = [[[at(b0, m, b1, a1) for b0 in range(2)] for a1 in range(2)]
                     for b1 in range(2)]
            result = jnp.dot(
                jnp.concatenate([left(near, spots[0]), left(near, spots[1])], axis=0),
                tiles(m), preferred_element_type=jnp.float32)
            for b1 in range(2):
                collect(found, spots[b1], result[
                    b1 * 4 * pair:(b1 + 1) * 4 * pair, b1 * LANES:(b1 + 1) * LANES])
        values = finish(jnp.concatenate(found, axis=0), odd_col, first)
        scatter(
            me_row, n_row, along_row, col_send, n_col - 1, 1, stay_col, move_col, col_weight, values,
            False)

    arrived(part_vm.at[pl.ds(0, peers // 2)], send_sem)

    @pl.when(me_col == 0)
    def _():
        mirrored()
        forward(False)

    @pl.when(me_col > 0)
    def _():
        forward(True)
        mirrored()

    total = row_send[me_col] + col_send[me_row]
    arrived(part_vm, p_sem)
    out_ref[...] = tree([total] + [part_vm[d] for d in range(peers)])
    arrived(part_vm, send_sem)


def per_device(vectors, tile_values, tile_rows, tile_cols, tile_scale, tile_count, scale_table):
    n_row = lax.axis_size("row")
    n_col = lax.axis_size("col")
    piece_len = vectors.shape[1]
    slots = tile_rows.shape[-1]
    groups = piece_len // LANES
    chunk = groups * NVEC
    depth = slots * NVEC
    x = vectors.reshape(NVEC, groups, LANES).transpose(1, 0, 2)
    w = tile_values.reshape(slots, TILE * TILE)
    dma = pltpu.SemaphoreType.DMA
    hbm = pl.BlockSpec(memory_space=pltpu.HBM)
    out = pl.pallas_call(
        functools.partial(kernel, n_row, n_col, slots, piece_len),
        out_shape=pltpu.VMEM((chunk, LANES), jnp.float32),
        in_specs=[hbm] * 5 + [pl.BlockSpec(memory_space=pltpu.SMEM), hbm],
        out_specs=pl.BlockSpec(memory_space=pltpu.VMEM),
        scratch_shapes=[
            pltpu.VMEM((n_col * groups, NVEC, LANES), jnp.bfloat16),
            pltpu.VMEM((n_row * groups, NVEC, LANES), jnp.bfloat16),
            pltpu.VMEM((slots, TILE * TILE), jnp.bfloat16),
            pltpu.VMEM((slots // 2, TILE, LANES), jnp.bfloat16),
            pltpu.SMEM((3,) + tile_rows.shape, jnp.int32),
            pltpu.SMEM(scale_table.shape, jnp.float32),
            pltpu.SMEM((2, slots), jnp.int32),
            pltpu.VMEM((depth, LANES), jnp.int32),
            pltpu.VMEM((depth, LANES), jnp.int32),
            pltpu.VMEM((depth, LANES), jnp.float32),
            pltpu.VMEM((depth, LANES), jnp.float32),
            pltpu.VMEM((2, 2 * chunk // (2 * NVEC), depth, LANES), jnp.float32),
            pltpu.VMEM((n_col, chunk, LANES), jnp.float32),
            pltpu.VMEM((n_row, chunk, LANES), jnp.float32),
            pltpu.VMEM((n_col + n_row - 2, chunk, LANES), jnp.float32),
            pltpu.SemaphoreType.REGULAR, dma, dma, dma, dma, dma, dma,
        ],
        compiler_params=pltpu.CompilerParams(collective_id=0, has_side_effects=True),
        name="lanczos",
    )(x, w, tile_rows, tile_cols, tile_scale, tile_count, scale_table)
    return out.reshape(groups, NVEC, LANES).transpose(1, 0, 2).reshape(NVEC, piece_len)


def solution(mesh):
    return jax.shard_map(
        per_device,
        mesh=mesh,
        in_specs=(
            P(None, ("row", "col")),
            P("row", "col", None, None),
            P("row", "col", None),
            P("row", "col", None),
            P("row", "col", None),
            P("row", "col"),
            P(),
        ),
        out_specs=P(None, ("row", "col")),
        check_vma=False,
    )
```
